128 devices in a mesh: region: 32 (over x, z, core), basis: 4 (over y).
Axes of the slice: x: 4, y: 4, z: 4, core: 2. Of those that a mesh axis runs over, the one named last changes fastest.
Arguments:
- observations: bfloat16 [1048576, 128], P(('region', 'basis')), may hold values from -3 to 4
- basis_values: bfloat16 [1048576, 1024], P(('region', 'basis')), as said below
- mixing: bfloat16 [1024, 1024], P('basis'), may hold values from -0.1875 to 0.1875
- pattern: int32 [8, 8], replicated, may hold values 0 or 1
- decays: float32 [32, 1024], P('region', 'basis'), may hold values from 0 to 1
- loadings: float32 [1024], P('basis'), may hold values from 0.3 to 3
Outputs:
- obs_grad: bfloat16 [1048576, 128], P(('region', 'basis'))
- attenuation_slope: float32 [32, 1024], P('region', 'basis')
The draws below stay inside these ranges and needn't reach their ends.
Inputs may be any that keep to these rules, and one draw needn't show every extreme that they name: `basis_values`: every entry lies within 3.5 / 32768 ** 0.5 of zero.
All inputs are finite; a program needn't handle non-finite values.
Results may differ from the reference program's by a relative error of at most 0.015.
Values may be sent and summed in bfloat16 or wider, within the bound.
No kernel may reach another device: no remote copies, remote signals or barrier semaphores. Data moves between devices by JAX's collectives and lax.ppermute only.
A program may use at most 128 MiB of HBM per device.

```python
import math
import jax
import jax.numpy as jnp
from jax import lax

M = 1024
BLOCK = 128
K = 128
ROWS_REG = 32768
TERRITORY_TOTAL = 32
OBS = 1048576
NBLK = 8


def row_rates(key, slow_share):
    keyring = jax.random.split(jax.random.fold_in(key, 101), 3)
    slow_mask = jax.random.uniform(keyring[0], (M,)) < slow_share
    slow_rate = jnp.log(5.0) / (1.4 * TERRITORY_TOTAL) * jax.random.uniform(keyring[1], (M,), minval=0.3, maxval=1.0)
    fast_rate = jnp.exp(jax.random.uniform(keyring[2], (M,), minval=jnp.log(0.12), maxval=jnp.log(0.7)))
    return (slow_mask, jnp.where(slow_mask, slow_rate, fast_rate))


def draw_decays(key, part):
    slow_share = 0.5
    slow_mask, background_intensity = row_rates(key, slow_share)
    keyring = jax.random.split(jax.random.fold_in(key, 202), 2)
    multiplier_entries = jax.random.uniform(keyring[0], (TERRITORY_TOTAL, M), minval=0.7, maxval=1.4)
    locale_position = jax.random.randint(keyring[1], (2,), 0, TERRITORY_TOTAL)
    pulse_occurrences = jnp.sum((jnp.arange(TERRITORY_TOTAL)[:, None] == locale_position[None, :]).astype(jnp.float32), axis=1)
    summed_intensity = background_intensity[None, :] * multiplier_entries + 0.35 * pulse_occurrences[:, None]
    return jnp.exp(-summed_intensity).astype(jnp.float32)


def draw_basis_values(key, part):
    slow_share = 0.5
    slow_mask, background_intensity = row_rates(key, slow_share)
    keyring = jax.random.split(jax.random.fold_in(key, 303), 2)
    slow_weight = jax.random.uniform(keyring[0], (M,), minval=0.05, maxval=0.15)
    column_weight = jnp.where(slow_mask, slow_weight, 3.0 * (1.0 - jnp.exp(-background_intensity)))
    fluctuation = jax.random.normal(keyring[1], (OBS, M), jnp.float32)
    spread_scale = 1.0 / jnp.sqrt(jnp.float32(ROWS_REG))
    values = fluctuation * spread_scale + column_weight[None, :] / jnp.float32(ROWS_REG)
    return jnp.clip(values, -3.5 * spread_scale, 3.5 * spread_scale).astype(jnp.bfloat16)


def draw_observations(key, part):
    keyring = jax.random.split(jax.random.fold_in(key, 404), 2)
    trait_level = jax.random.uniform(keyring[0], (K,), minval=0.5, maxval=1.0)
    fluctuation = jax.random.normal(keyring[1], (OBS, K), jnp.float32)
    return jnp.clip(trait_level[None, :] + fluctuation, -3.0, 4.0).astype(jnp.bfloat16)


def place_ends(entries, rng, smallest, largest):
    dims = entries.shape
    place = [jax.random.randint(jax.random.fold_in(rng, axis), (), 0, dims[axis]) for axis in range(len(dims))]
    entries = entries.at[tuple(place)].set(smallest)
    longest = dims.index(max(dims))
    place[longest] = (place[longest] + 1) % dims[longest]
    return entries.at[tuple(place)].set(largest)


def level_of(key, extent, shards, low, top_value):
    level = 1.0
    for axis_at, parts in shards:
        draws = jax.random.uniform(jax.random.fold_in(jax.random.fold_in(key, 6), axis_at), (parts,), jnp.float32, low / len(shards), top_value / len(shards))
        level = level * jnp.repeat(jnp.exp(draws), extent[axis_at] // parts).reshape((-1,) + (1,) * (len(extent) - 1 - axis_at))
    return level


def noise(rng, dims, width, limit, shards=(), held_as=jnp.bfloat16):
    array = jax.random.normal(rng, dims, jnp.float32) * width
    if len(shards) > 0:
        array = level_of(rng, dims, shards, -0.22, 0.18) * array
    return jnp.clip(array, min=-limit, max=limit).astype(held_as)


def setup_inputs(seed: int = 0) -> dict:
    splits = jax.random.split(jax.random.key(seed), 7)
    return {
        "observations": draw_observations(jax.random.fold_in(splits[6], 71), 0),
        "basis_values": draw_basis_values(jax.random.fold_in(splits[6], 71), 0),
        "mixing": noise(splits[2], (M, M), M ** -0.5, 0.1875, ((0, 4),)),
        "pattern": place_ends((jax.random.randint(splits[3], (NBLK, NBLK), 0, 2) < 1).astype(jnp.int32), jax.random.fold_in(splits[3], 1), 0, 1),
        "decays": draw_decays(jax.random.fold_in(splits[6], 71), 0),
        "loadings": jnp.clip(jnp.exp(math.log(3.0) - 2.3025851 * jax.random.uniform(splits[5], (M,), jnp.float32) ** level_of(splits[5], (M,), ((0, 4),), -0.2, 0.2)), 0.3, 3.0),
    }


def contract_rows(first_operand, second_operand):
    return lax.dot_general(first_operand, second_operand, (((0,), (0,)), ((), ())), preferred_element_type=jnp.float32)


def block_matrix(mixing, pattern):
    blocks = jnp.arange(M) // BLOCK
    onehot = (blocks[:, None] == jnp.arange(NBLK)[None, :]).astype(jnp.float32)
    expanded = jnp.dot(jnp.dot(onehot, pattern.astype(jnp.float32)), onehot.T)
    return (jnp.eye(M, dtype=jnp.float32) + mixing.astype(jnp.float32) * expanded).astype(jnp.bfloat16)


def reference(observations, basis_values, mixing, pattern, decays, loadings):
    basis_rows = basis_values.reshape(TERRITORY_TOTAL, ROWS_REG, M)
    targets = observations.reshape(TERRITORY_TOTAL, ROWS_REG, K)
    mixer_matrix = block_matrix(mixing, pattern)

    def project_up(pairing):
        return contract_rows(pairing[0], pairing[1])

    def predict(pairing):
        return jnp.dot(pairing[0], pairing[1], preferred_element_type=jnp.float32)

    def mix_one(column):
        return jnp.dot(mixer_matrix, column, preferred_element_type=jnp.float32)

    def mix_back(column):
        return contract_rows(mixer_matrix, column)

    summary = lax.map(project_up, (basis_rows, targets)).astype(jnp.bfloat16)
    mixed_terms = lax.map(mix_one, summary)

    def upward(carried, inputs):
        factor, addend = inputs
        return factor[:, None] * carried + addend, carried

    zero_state = jnp.zeros((M, K), jnp.float32)
    _, previous = lax.scan(upward, zero_state, (decays, mixed_terms))
    states = decays[:, :, None] * previous + mixed_terms
    loaded_values = (loadings[None, :, None] * states).astype(jnp.bfloat16)
    fitted = lax.map(predict, (basis_rows, loaded_values))
    residual = (fitted - targets.astype(jnp.float32)).astype(jnp.bfloat16)
    pulled = loadings[None, :, None] * lax.map(project_up, (basis_rows, residual))

    def downward(carried, inputs):
        factor, addend = inputs
        adjoint = addend + carried
        return factor[:, None] * adjoint, adjoint

    _, adjoints = lax.scan(downward, zero_state, (decays, pulled), reverse=True)
    attenuation_slope = jnp.sum(adjoints * previous, axis=2) / K
    adjoint_b = adjoints.astype(jnp.bfloat16)
    back_mixed = lax.map(mix_back, adjoint_b).astype(jnp.bfloat16)
    spread = lax.map(predict, (basis_rows, back_mixed))
    obs_grad = (spread - residual.astype(jnp.float32)).astype(jnp.bfloat16).reshape(OBS, K)
    return obs_grad, attenuation_slope
```

```python
import functools

import jax
import jax.numpy as jnp
from jax import lax
from jax.experimental import pallas as pl
from jax.experimental.pallas import tpu as pltpu
from jax.sharding import PartitionSpec as P

BLOCK = 128
LANES = 128
TILE_ROWS = 1024
VMEM_LIMIT = 56 * 1024 * 1024
ALL = ("region", "basis")
F32 = jnp.float32
BF16 = jnp.bfloat16


def split(value):
    high = value.astype(BF16)
    return high, (value - high.astype(F32)).astype(BF16)


def compiler_params():
    return pltpu.CompilerParams(
        dimension_semantics=("arbitrary",), vmem_limit_bytes=VMEM_LIMIT
    )


def contract_rows(first, second):
    return lax.dot_general(first, second, (((0,), (0,)), ((), ())), preferred_element_type=F32)


def contract_lanes(first, second):
    return lax.dot_general(first, second, (((1,), (1,)), ((), ())), preferred_element_type=F32)


def store_by_trait(total, spread, message):
    traits, width = total.shape
    groups = width // LANES
    for s in range(groups):
        spread[pl.ds(s, traits, stride=groups), :] = total[:, s * LANES : (s + 1) * LANES]
    message[:, 0:groups, :] = spread[...].reshape(traits, groups, LANES).astype(BF16)


def load_by_trait(message, spread, target, at):
    traits = message.shape[0]
    groups = target.shape[1] // LANES
    spread[...] = message[:, 0:groups, :].astype(F32).reshape(traits * groups, LANES)
    for s in range(groups):
        target[at : at + traits, s * LANES : (s + 1) * LANES] = spread[
            pl.ds(s, traits, stride=groups), :
        ].astype(BF16)


def summary_kernel(phi, y, rates, loads, message, total, spread):
    step = pl.program_id(0)

    @pl.when(step == 0)
    def _():
        total[...] = jnp.zeros_like(total)

    total[...] += contract_rows(y[...], phi[...])

    @pl.when(step == pl.num_programs(0) - 1)
    def _():
        store_by_trait(total[...], spread, message)
        groups = total.shape[1] // LANES
        pieces = []
        for vector in (rates, loads):
            width = vector.shape[1] // LANES
            parts = [split(vector[:, h * LANES : (h + 1) * LANES]) for h in range(width)]
            pieces += [part[0] for part in parts] + [part[1] for part in parts]
        tail = jnp.concatenate([piece.astype(F32) for piece in pieces], axis=0).astype(BF16)
        message[:, groups : groups + tail.shape[0], :] = jnp.broadcast_to(
            tail[None], (message.shape[0],) + tail.shape
        )


def forward_kernel(
    count, message, mixing, pattern, reply, previous, rates, loads, wide, tiles
):
    devices, rows, _ = message.shape
    owners = devices // count
    groups = mixing.shape[0] // LANES
    halves = groups // owners
    wide[...] = message[...].astype(F32).reshape(devices * rows, LANES)
    step = owners * rows

    def column(row):
        return wide[pl.ds(row, count, stride=step), :]

    summary = []
    for s in range(groups):
        block = column(s)
        for b in range(1, owners):
            block = block + column(b * rows + s)
        summary.append(block.astype(BF16))
    summary = jnp.concatenate(summary, axis=1)
    for b in range(owners):
        for h in range(halves):
            at = b * rows + groups + h
            rates_block = column(at) + column(at + halves)
            tiles[pl.ds(b * halves + h, count, stride=groups), :] = rates_block
    rates[...] = tiles[...].reshape(count, groups, LANES)
    load_rows = []
    for b in range(owners):
        for h in range(halves):
            at = b * rows + groups + 2 * halves + h
            load_rows.append(wide[at : at + 1, :] + wide[at + halves : at + halves + 1, :])
    loads[...] = jnp.concatenate(load_rows, axis=0)
    mask = pattern[...]
    for s in range(groups):
        kept = (summary.astype(F32) * mask[s : s + 1, :]).astype(BF16)
        product = contract_lanes(kept, mixing[s * LANES : (s + 1) * LANES, :])
        tiles[pl.ds(s, count, stride=groups), :] = product + summary[
            :, s * LANES : (s + 1) * LANES
        ].astype(F32)
    carried = jnp.zeros((groups, LANES), F32)
    scale = loads[...]
    for r in range(count):
        previous[r] = carried
        carried = rates[r] * carried + tiles[r * groups : (r + 1) * groups, :]
        value = (scale * carried).astype(BF16)
        for b in range(owners):
            reply[r * owners + b] = value


def residual_kernel(phi, y, arrived, message, weights, total, spread):
    step = pl.program_id(0)

    @pl.when(step == 0)
    def _():
        total[...] = jnp.zeros_like(total)
        load_by_trait(arrived, spread, weights, 0)

    fitted = contract_lanes(phi[...], weights[...])
    residual = (fitted - y[...].astype(F32)).astype(BF16)
    total[...] += contract_rows(residual, phi[...])

    @pl.when(step == pl.num_programs(0) - 1)
    def _():
        store_by_trait(total[...], spread, message)


def backward_kernel(
    count, traits, message, mixing, pattern, previous, rates, loads, reply, tiles
):
    devices = message.shape[0]
    owners = devices // count
    groups = mixing.shape[0] // LANES
    halves = groups // owners
    scale = loads[...]
    adjoint = jnp.zeros((groups, LANES), F32)
    for r in reversed(range(count)):
        pulled = message[r * owners].astype(F32)
        for b in range(1, owners):
            pulled = pulled + message[r * owners + b].astype(F32)
        pulled = scale * pulled
        if r + 1 < count:
            adjoint = pulled + rates[r + 1] * adjoint
        else:
            adjoint = pulled
        tiles[r * groups : (r + 1) * groups, :] = adjoint
        slope = adjoint * previous[r] * (1.0 / traits)
        high, low = split(slope)
        high, low = high.astype(F32), low.astype(F32)
        for b in range(owners):
            mine = slice(b * halves, (b + 1) * halves)
            tail = jnp.concatenate(
                [high[mine], low[mine], jnp.zeros((groups - 2 * halves, LANES), F32)], axis=0
            )
            reply[r * owners + b, groups : 2 * groups, :] = tail.astype(BF16)
    blocks = [tiles[pl.ds(s, count, stride=groups), :].astype(BF16) for s in range(groups)]
    adjoints = jnp.concatenate(blocks, axis=1)
    mask = pattern[...]
    for s in range(groups):
        kept = (adjoints.astype(F32) * mask[s : s + 1, :]).astype(BF16)
        product = jnp.dot(
            kept, mixing[:, s * LANES : (s + 1) * LANES], preferred_element_type=F32
        )
        tiles[pl.ds(s, count, stride=groups), :] = product + blocks[s].astype(F32)
    for r in range(count):
        back = tiles[r * groups : (r + 1) * groups, :].astype(BF16)
        for b in range(owners):
            reply[r * owners + b, 0:groups, :] = back


def gradient_kernel(halves, phi, y, loaded, arrived, out, slope, weights, spread):
    traits = loaded.shape[0]
    groups = weights.shape[1] // LANES

    @pl.when(pl.program_id(0) == 0)
    def _():
        load_by_trait(arrived, spread, weights, 0)
        load_by_trait(loaded, spread, weights, traits)
        tail = jnp.sum(arrived[:, groups : 2 * groups, :].astype(F32), axis=0)
        for h in range(halves):
            slope[:, h * LANES : (h + 1) * LANES] = (
                tail[h : h + 1, :] + tail[halves + h : halves + h + 1, :]
            )

    both = contract_lanes(phi[...], weights[...])
    residual = (both[:, traits:] - y[...].astype(F32)).astype(BF16)
    out[...] = (both[:, :traits] - residual.astype(F32)).astype(BF16)


def shards(count, observations, basis_values, mixing, pattern, decays, loadings):
    devices = lax.axis_size("region") * lax.axis_size("basis")
    rows, width = basis_values.shape
    traits = observations.shape[1]
    groups = width // LANES
    share = decays.shape[1]
    halves = share // LANES
    tile = min(TILE_ROWS, rows)
    grid = (rows // tile,)
    mixing_all = lax.all_gather(mixing, "basis", axis=0, tiled=True)
    expanded = jnp.repeat(pattern.astype(F32), BLOCK, axis=1)
    expanded_t = jnp.repeat(pattern.T.astype(F32), BLOCK, axis=1)

    def block(shape):
        return pl.BlockSpec(shape, lambda i: (0,) * len(shape))

    phi_spec = pl.BlockSpec((tile, width), lambda i: (i, 0))
    y_spec = pl.BlockSpec((tile, traits), lambda i: (i, 0))
    total = pltpu.VMEM((traits, width), F32)
    spread = pltpu.VMEM((traits * groups, LANES), F32)
    tiles = pltpu.VMEM((count * groups, LANES), F32)

    def exchange(value):
        return lax.all_to_all(value, ALL, 0, 0, tiled=True)

    sums = pl.pallas_call(
        summary_kernel,
        grid=grid,
        in_specs=[phi_spec, y_spec, block((1, share)), block((1, share))],
        out_specs=block((traits, 2 * groups, LANES)),
        out_shape=jax.ShapeDtypeStruct((traits, 2 * groups, LANES), BF16),
        scratch_shapes=[total, spread],
        compiler_params=compiler_params(),
        name="summary",
    )(basis_values, observations, decays, loadings[None, :])
    sums = exchange(sums)
    loaded, previous, rates, loads = pl.pallas_call(
        functools.partial(forward_kernel, count),
        out_shape=(
            jax.ShapeDtypeStruct((devices, groups, LANES), BF16),
            jax.ShapeDtypeStruct((count, groups, LANES), F32),
            jax.ShapeDtypeStruct((count, groups, LANES), F32),
            jax.ShapeDtypeStruct((groups, LANES), F32),
        ),
        scratch_shapes=[pltpu.VMEM((devices * 2 * groups, LANES), F32), tiles],
        compiler_params=pltpu.CompilerParams(vmem_limit_bytes=VMEM_LIMIT),
        name="forward",
    )(sums, mixing_all, expanded)
    loaded = exchange(loaded)
    pulled = pl.pallas_call(
        residual_kernel,
        grid=grid,
        in_specs=[phi_spec, y_spec, block((traits, groups, LANES))],
        out_specs=block((traits, groups, LANES)),
        out_shape=jax.ShapeDtypeStruct((traits, groups, LANES), BF16),
        scratch_shapes=[pltpu.VMEM((traits, width), BF16), total, spread],
        compiler_params=compiler_params(),
        name="residual",
    )(basis_values, observations, loaded)
    pulled = exchange(pulled)
    back = pl.pallas_call(
        functools.partial(backward_kernel, count, traits),
        out_shape=jax.ShapeDtypeStruct((devices, 2 * groups, LANES), BF16),
        scratch_shapes=[tiles],
        compiler_params=pltpu.CompilerParams(vmem_limit_bytes=VMEM_LIMIT),
        name="backward",
    )(pulled, mixing_all, expanded_t, previous, rates, loads)
    back = exchange(back)
    obs_grad, slope = pl.pallas_call(
        functools.partial(gradient_kernel, halves),
        grid=grid,
        in_specs=[
            phi_spec,
            y_spec,
            block((traits, groups, LANES)),
            block((traits, 2 * groups, LANES)),
        ],
        out_specs=(y_spec, block((1, share))),
        out_shape=(
            jax.ShapeDtypeStruct((rows, traits), BF16),
            jax.ShapeDtypeStruct((1, share), F32),
        ),
        scratch_shapes=[pltpu.VMEM((2 * traits, width), BF16), spread],
        compiler_params=compiler_params(),
        name="gradient",
    )(basis_values, observations, loaded, back)
    return obs_grad, slope


def solution(mesh):
    in_specs = (
        P(ALL, None),
        P(ALL, None),
        P("basis", None),
        P(),
        P("region", "basis"),
        P("basis"),
    )
    out_specs = (P(ALL, None), P("region", "basis"))
    body = functools.partial(shards, mesh.shape["region"])
    return jax.shard_map(body, mesh=mesh, in_specs=in_specs, out_specs=out_specs, check_vma=False)
```

```python
import functools

import jax
import jax.numpy as jnp
from jax import lax
from jax.experimental import pallas as pl
from jax.experimental.pallas import tpu as pltpu
from jax.sharding import PartitionSpec as P

BLOCK = 128
LANES = 128
TILE_ROWS = 1024
VMEM_LIMIT = 48 * 1024 * 1024
ALL = ("region", "basis")
F32 = jnp.float32
BF16 = jnp.bfloat16
OWNERS = 4


def split(value):
    high = value.astype(BF16)
    return high, (value - high.astype(F32)).astype(BF16)


def start_chunks(tile, pairs, sems):
    rows = pairs[0][0].shape[0]
    chunks = []
    for i in range(rows // tile):
        at = pl.ds(i * tile, tile)
        copies = [
            pltpu.make_async_copy(source.at[at], target.at[at], sems.at[k, i])
            for k, (source, target) in enumerate(pairs)
        ]
        for copy in copies:
            copy.start()
        chunks.append((at, copies))
    return chunks


def wait_all(copies):
    for copy in copies:
        copy.wait()


def start_mixing(pieces, mixing, sems):
    own, near, far, near_other, far_other = pieces
    share, part = own.shape[0], far.shape[0]
    owner = lax.axis_index("basis")
    core = lax.rem(lax.axis_index("region"), 2)
    across = lax.rem(owner + 2, OWNERS) * share
    starts = (
        owner * share,
        lax.rem(owner + 3 + 2 * core, OWNERS) * share,
        across + core * part,
        lax.rem(owner + 1 + 2 * core, OWNERS) * share,
        across + (1 - core) * part,
    )
    copies = []
    for k, (piece, start) in enumerate(zip(pieces, starts)):
        at = pl.ds(pl.multiple_of(start, part), piece.shape[0])
        copies.append(pltpu.make_async_copy(piece, mixing.at[at], sems.at[k]))
        copies[-1].start()
    return copies


def keep(blocks, present):
    return jnp.concatenate(
        [(block * flag.astype(F32)).astype(BF16) for block, flag in zip(blocks, present)], axis=1
    )


def contract_lanes(first, second):
    return lax.dot_general(first, second, (((1,), (1,)), ((), ())), preferred_element_type=F32)


def store_by_trait(total, spread, message):
    traits, width = total.shape
    groups = width // LANES
    for s in range(groups):
        spread[pl.ds(s, traits, stride=groups), :] = total[:, s * LANES : (s + 1) * LANES]
    message[:, 0:groups, :] = spread[...].reshape(traits, groups, LANES).astype(BF16)


def load_by_trait(message, spread, target, at):
    traits = message.shape[0]
    groups = target.shape[1] // LANES
    spread[...] = message[:, 0:groups, :].astype(F32).reshape(traits * groups, LANES)
    for s in range(groups):
        target[at : at + traits, s * LANES : (s + 1) * LANES] = spread[
            pl.ds(s, traits, stride=groups), :
        ].astype(BF16)


def summary_kernel(tile, phi, y, rates, loads, message, phi_here, y_here, total, spread, sems):
    chunks = start_chunks(tile, ((y, y_here), (phi, phi_here)), sems)
    for i, (at, copies) in enumerate(chunks):
        wait_all(copies)
        product = jnp.dot(y_here[at, :].T, phi_here[at, :], preferred_element_type=F32)
        if i == 0:
            total[...] = product
        else:
            total[...] += product
    store_by_trait(total[...], spread, message)
    groups = total.shape[1] // LANES
    pieces = []
    for vector in (rates, loads):
        width = vector.shape[1] // LANES
        parts = [split(vector[:, h * LANES : (h + 1) * LANES]) for h in range(width)]
        pieces += [part[0] for part in parts] + [part[1] for part in parts]
    tail = jnp.concatenate([piece.astype(F32) for piece in pieces], axis=0).astype(BF16)
    message[:, groups : groups + tail.shape[0], :] = jnp.broadcast_to(
        tail[None], (message.shape[0],) + tail.shape
    )


def forward_kernel(count, message, pattern, *refs):
    *pieces, reply, previous, rates, loads, mixing, wide, tiles, sems = refs
    copies = start_mixing(pieces, mixing, sems)
    devices, rows, _ = message.shape
    owners = devices // count
    groups = mixing.shape[0] // LANES
    halves = groups // owners
    wide[...] = message[...].astype(F32).reshape(devices * rows, LANES)
    step = owners * rows

    def column(row):
        return wide[pl.ds(row, count, stride=step), :]

    summary = []
    for s in range(groups):
        block = column(s)
        for b in range(1, owners):
            block = block + column(b * rows + s)
        summary.append(block.astype(BF16).astype(F32))
    for b in range(owners):
        for h in range(halves):
            at = b * rows + groups + h
            rates_block = column(at) + column(at + halves)
            tiles[pl.ds(b * halves + h, count, stride=groups), :] = rates_block
    rates[...] = tiles[...].reshape(count, groups, LANES)
    load_rows = []
    for b in range(owners):
        for h in range(halves):
            at = b * rows + groups + 2 * halves + h
            load_rows.append(wide[at : at + 1, :] + wide[at + halves : at + halves + 1, :])
    loads[...] = jnp.concatenate(load_rows, axis=0)
    wait_all(copies)
    for s in range(groups):
        kept = keep(summary, [pattern[s, k] for k in range(groups)])
        product = contract_lanes(kept, mixing[s * LANES : (s + 1) * LANES, :])
        tiles[pl.ds(s, count, stride=groups), :] = product + summary[s]
    carried = jnp.zeros((groups, LANES), F32)
    scale = loads[...]
    for r in range(count):
        previous[r] = carried
        carried = rates[r] * carried + tiles[r * groups : (r + 1) * groups, :]
        value = (scale * carried).astype(BF16)
        for b in range(owners):
            reply[r * owners + b] = value


def residual_kernel(
    tile, phi, y, arrived, message, phi_here, y_here, weights, total, spread, sems
):
    chunks = start_chunks(tile, ((y, y_here), (phi, phi_here)), sems)
    load_by_trait(arrived, spread, weights, 0)
    for i, (at, copies) in enumerate(chunks):
        wait_all(copies)
        fitted = contract_lanes(weights[...], phi_here[at, :])
        residual = (fitted - y_here[at, :].T.astype(F32)).astype(BF16)
        product = jnp.dot(residual, phi_here[at, :], preferred_element_type=F32)
        if i == 0:
            total[...] = product
        else:
            total[...] += product
    store_by_trait(total[...], spread, message)


def backward_kernel(count, traits, message, pattern, previous, rates, loads, *refs):
    *pieces, reply, mixing, tiles, sems = refs
    copies = start_mixing(pieces, mixing, sems)
    devices = message.shape[0]
    owners = devices // count
    groups = mixing.shape[0] // LANES
    halves = groups // owners
    scale = loads[...]
    adjoint = jnp.zeros((groups, LANES), F32)
    for r in reversed(range(count)):
        pulled = message[r * owners].astype(F32)
        for b in range(1, owners):
            pulled = pulled + message[r * owners + b].astype(F32)
        pulled = scale * pulled
        if r + 1 < count:
            adjoint = pulled + rates[r + 1] * adjoint
        else:
            adjoint = pulled
        tiles[r * groups : (r + 1) * groups, :] = adjoint
        slope = adjoint * previous[r] * (1.0 / traits)
        high, low = split(slope)
        high, low = high.astype(F32), low.astype(F32)
        for b in range(owners):
            mine = slice(b * halves, (b + 1) * halves)
            tail = jnp.concatenate(
                [high[mine], low[mine], jnp.zeros((groups - 2 * halves, LANES), F32)], axis=0
            )
            reply[r * owners + b, groups : 2 * groups, :] = tail.astype(BF16)
    blocks = [
        tiles[pl.ds(s, count, stride=groups), :].astype(BF16).astype(F32) for s in range(groups)
    ]
    wait_all(copies)
    for s in range(groups):
        kept = keep(blocks, [pattern[k, s] for k in range(groups)])
        product = jnp.dot(
            kept, mixing[:, s * LANES : (s + 1) * LANES], preferred_element_type=F32
        )
        tiles[pl.ds(s, count, stride=groups), :] = product + blocks[s]
    for r in range(count):
        back = tiles[r * groups : (r + 1) * groups, :].astype(BF16)
        for b in range(owners):
            reply[r * owners + b, 0:groups, :] = back


def gradient_kernel(
    tile,
    halves,
    phi,
    y,
    loaded,
    arrived,
    out,
    slope,
    phi_here,
    y_here,
    out_here,
    weights,
    spread,
    sems,
):
    chunks = start_chunks(tile, ((y, y_here), (phi, phi_here)), sems)
    traits = loaded.shape[0]
    groups = weights.shape[1] // LANES
    load_by_trait(arrived, spread, weights, 0)
    load_by_trait(loaded, spread, weights, traits)
    tail = jnp.sum(arrived[:, groups : 2 * groups, :].astype(F32), axis=0)
    for h in range(halves):
        slope[:, h * LANES : (h + 1) * LANES] = (
            tail[h : h + 1, :] + tail[halves + h : halves + h + 1, :]
        )
    stores = []
    for i, (at, copies) in enumerate(chunks):
        wait_all(copies)
        both = contract_lanes(weights[...], phi_here[at, :])
        residual = (both[traits:] - y_here[at, :].T.astype(F32)).astype(BF16)
        out_here[at, :] = (both[:traits] - residual.astype(F32)).astype(BF16).T
        stores.append(pltpu.make_async_copy(out_here.at[at], out.at[at], sems.at[2, i]))
        stores[-1].start()
    wait_all(stores)


def mixing_pieces(mixing):
    regions = lax.axis_size("region")
    part = mixing.shape[0] // 2
    core = lax.rem(lax.axis_index("region"), 2)
    half = lax.dynamic_slice_in_dim(mixing, core * part, part, 0)

    def move(value, target):
        pairs = [
            (r * OWNERS + b, target(r, b)) for r in range(regions) for b in range(OWNERS)
        ]
        return lax.ppermute(value, ALL, pairs)

    def beside(r, b):
        return r * OWNERS + (b + 1 + 2 * (r % 2)) % OWNERS

    def across(r, b):
        return r * OWNERS + (b + 2) % OWNERS

    def other_core(r, b):
        return (r ^ 1) * OWNERS + b

    def swap(near, far):
        return mixing, near, far, move(near, other_core), move(far, other_core)

    return (move(mixing, beside), move(half, across)), swap


def shards(count, observations, basis_values, mixing, pattern, decays, loadings):
    devices = lax.axis_size("region") * lax.axis_size("basis")
    rows, width = basis_values.shape
    traits = observations.shape[1]
    groups = width // LANES
    share = decays.shape[1]
    halves = share // LANES
    tile = min(TILE_ROWS, rows)
    chunks = rows // tile
    fetched, swap = mixing_pieces(mixing)

    hbm = pl.BlockSpec(memory_space=pl.ANY)
    vmem = pl.BlockSpec(memory_space=pltpu.VMEM)
    smem = pl.BlockSpec(memory_space=pltpu.SMEM)
    params = pltpu.CompilerParams(vmem_limit_bytes=VMEM_LIMIT)
    phi_here = pltpu.VMEM((rows, width), BF16)
    y_here = pltpu.VMEM((rows, traits), BF16)
    total = pltpu.VMEM((traits, width), F32)
    spread = pltpu.VMEM((traits * groups, LANES), F32)
    tiles = pltpu.VMEM((count * groups, LANES), F32)
    mixing_here = pltpu.VMEM((width, width), BF16)
    short = jax.ShapeDtypeStruct((devices, groups, LANES), BF16)
    long = jax.ShapeDtypeStruct((devices, 2 * groups, LANES), BF16)

    def sems(*shape):
        return pltpu.SemaphoreType.DMA(shape)

    def exchange(value):
        return lax.all_to_all(value, ALL, 0, 0, tiled=True)

    sums = pl.pallas_call(
        functools.partial(summary_kernel, tile),
        in_specs=[hbm, hbm, vmem, vmem],
        out_specs=vmem,
        out_shape=long,
        scratch_shapes=[phi_here, y_here, total, spread, sems(2, chunks)],
        compiler_params=params,
        name="summary",
    )(basis_values, observations, decays, loadings[None, :])
    sums, fetched = lax.optimization_barrier((sums, fetched))
    pieces = swap(*fetched)
    sums = exchange(sums)
    loaded, previous, rates, loads = pl.pallas_call(
        functools.partial(forward_kernel, count),
        in_specs=[vmem, smem] + [hbm] * len(pieces),
        out_specs=(vmem,) * 4,
        out_shape=(
            short,
            jax.ShapeDtypeStruct((count, groups, LANES), F32),
            jax.ShapeDtypeStruct((count, groups, LANES), F32),
            jax.ShapeDtypeStruct((groups, LANES), F32),
        ),
        scratch_shapes=[
            mixing_here,
            pltpu.VMEM((devices * 2 * groups, LANES), F32),
            tiles,
            sems(len(pieces)),
        ],
        compiler_params=params,
        name="forward",
    )(sums, pattern, *pieces)
    loaded = exchange(loaded)
    pulled = pl.pallas_call(
        functools.partial(residual_kernel, tile),
        in_specs=[hbm, hbm, vmem],
        out_specs=vmem,
        out_shape=short,
        scratch_shapes=[
            phi_here,
            y_here,
            pltpu.VMEM((traits, width), BF16),
            total,
            spread,
            sems(2, chunks),
        ],
        compiler_params=params,
        name="residual",
    )(basis_values, observations, loaded)
    pulled = exchange(pulled)
    back = pl.pallas_call(
        functools.partial(backward_kernel, count, traits),
        in_specs=[vmem, smem, vmem, vmem, vmem] + [hbm] * len(pieces),
        out_specs=vmem,
        out_shape=long,
        scratch_shapes=[mixing_here, tiles, sems(len(pieces))],
        compiler_params=params,
        name="backward",
    )(pulled, pattern, previous, rates, loads, *pieces)
    back = exchange(back)
    obs_grad, slope = pl.pallas_call(
        functools.partial(gradient_kernel, tile, halves),
        in_specs=[hbm, hbm, vmem, vmem],
        out_specs=(hbm, vmem),
        out_shape=(
            jax.ShapeDtypeStruct((rows, traits), BF16),
            jax.ShapeDtypeStruct((1, share), F32),
        ),
        scratch_shapes=[
            phi_here,
            y_here,
            y_here,
            pltpu.VMEM((2 * traits, width), BF16),
            spread,
            sems(3, chunks),
        ],
        compiler_params=params,
        name="gradient",
    )(basis_values, observations, loaded, back)
    return obs_grad, slope


def solution(mesh):
    in_specs = (
        P(ALL, None),
        P(ALL, None),
        P("basis", None),
        P(),
        P("region", "basis"),
        P("basis"),
    )
    out_specs = (P(ALL, None), P("region", "basis"))
    body = functools.partial(shards, mesh.shape["region"])
    return jax.shard_map(body, mesh=mesh, in_specs=in_specs, out_specs=out_specs, check_vma=False)
```

```python
import functools

import jax
import jax.numpy as jnp
from jax import lax
from jax.experimental import pallas as pl
from jax.experimental.pallas import tpu as pltpu
from jax.sharding import PartitionSpec as P

BLOCK = 128
LANES = 128
TILE_ROWS = 1024
MIB = 1024 * 1024
ALL = ("region", "basis")
F32 = jnp.float32
BF16 = jnp.bfloat16
OWNERS = 4


def split(value):
    high = value.astype(BF16)
    return high, (value - high.astype(F32)).astype(BF16)


def start_chunks(tile, pairs, sems):
    rows = pairs[0][0].shape[0]
    chunks = []
    for i in range(rows // tile):
        at = pl.ds(i * tile, tile)
        copies = [
            pltpu.make_async_copy(source.at[at], target.at[at], sems.at[k, i])
            for k, (source, target) in enumerate(pairs)
        ]
        for copy in copies:
            copy.start()
        chunks.append((at, copies))
    return chunks


def wait_all(copies):
    for copy in copies:
        copy.wait()


def start_mixing(pieces, mixing, sems):
    share = pieces[0].shape[0]
    owner = lax.axis_index("basis")
    core = lax.rem(lax.axis_index("region"), 2)
    shifts = (0, 3 + 2 * core, 1 + 2 * core, 2)
    copies = []
    for k, (piece, shift) in enumerate(zip(pieces, shifts)):
        start = pl.multiple_of(lax.rem(owner + shift, OWNERS) * share, share)
        copies.append(pltpu.make_async_copy(piece, mixing.at[pl.ds(start, share)], sems.at[k]))
        copies[-1].start()
    return copies


def keep(blocks, present):
    return jnp.concatenate(
        [(block * flag.astype(F32)).astype(BF16) for block, flag in zip(blocks, present)], axis=1
    )


def contract_lanes(first, second):
    return lax.dot_general(first, second, (((1,), (1,)), ((), ())), preferred_element_type=F32)


def store_by_trait(total, spread, message):
    traits, width = total.shape
    groups = width // LANES
    for s in range(groups):
        spread[pl.ds(s, traits, stride=groups), :] = total[:, s * LANES : (s + 1) * LANES]
    message[:, 0:groups, :] = spread[...].reshape(traits, groups, LANES).astype(BF16)


def load_by_trait(message, spread, target, at):
    traits = message.shape[0]
    groups = target.shape[1] // LANES
    spread[...] = message[:, 0:groups, :].astype(F32).reshape(traits * groups, LANES)
    for s in range(groups):
        target[at : at + traits, s * LANES : (s + 1) * LANES] = spread[
            pl.ds(s, traits, stride=groups), :
        ].astype(BF16)


def summary_kernel(
    tile,
    phi,
    y,
    rates_away,
    loads_away,
    message,
    phi_here,
    y_here,
    rates,
    loads,
    total,
    spread,
    sems,
    small_sems,
):
    small = (
        pltpu.make_async_copy(rates_away, rates, small_sems.at[0]),
        pltpu.make_async_copy(loads_away, loads, small_sems.at[1]),
    )
    chunks = start_chunks(tile, ((y, y_here), (phi, phi_here)), sems)
    for copy in small:
        copy.start()
    for i, (at, copies) in enumerate(chunks):
        wait_all(copies)
        product = jnp.dot(y_here[at, :].T, phi_here[at, :], preferred_element_type=F32)
        if i == 0:
            total[...] = product
        else:
            total[...] += product
    store_by_trait(total[...], spread, message)
    wait_all(small)
    groups = total.shape[1] // LANES
    pieces = []
    for vector in (rates, loads):
        width = vector.shape[1] // LANES
        parts = [split(vector[:, h * LANES : (h + 1) * LANES]) for h in range(width)]
        pieces += [part[0] for part in parts] + [part[1] for part in parts]
    tail = jnp.concatenate([piece.astype(F32) for piece in pieces], axis=0).astype(BF16)
    message[:, groups : groups + tail.shape[0], :] = jnp.broadcast_to(
        tail[None], (message.shape[0],) + tail.shape
    )


def forward_kernel(count, message, pattern, *refs):
    *pieces, reply, previous, rates, loads, mixing, wide, tiles, sems = refs
    copies = start_mixing(pieces, mixing, sems)
    devices, rows, _ = message.shape
    owners = devices // count
    groups = mixing.shape[0] // LANES
    halves = groups // owners
    wide[...] = message[...].astype(F32).reshape(devices * rows, LANES)
    step = owners * rows

    def column(row):
        return wide[pl.ds(row, count, stride=step), :]

    summary = []
    for s in range(groups):
        block = column(s)
        for b in range(1, owners):
            block = block + column(b * rows + s)
        summary.append(block.astype(BF16).astype(F32))
    for b in range(owners):
        for h in range(halves):
            at = b * rows + groups + h
            rates_block = column(at) + column(at + halves)
            tiles[pl.ds(b * halves + h, count, stride=groups), :] = rates_block
    rates[...] = tiles[...].reshape(count, groups, LANES)
    load_rows = []
    for b in range(owners):
        for h in range(halves):
            at = b * rows + groups + 2 * halves + h
            load_rows.append(wide[at : at + 1, :] + wide[at + halves : at + halves + 1, :])
    loads[...] = jnp.concatenate(load_rows, axis=0)
    wait_all(copies)
    for s in range(0, groups, 2):
        kept = [keep(summary, [pattern[t, k] for k in range(groups)]) for t in (s, s + 1)]
        product = contract_lanes(
            jnp.concatenate(kept, axis=0), mixing[s * LANES : (s + 2) * LANES, :]
        )
        tiles[pl.ds(s, count, stride=groups), :] = product[:count, :LANES] + summary[s]
        tiles[pl.ds(s + 1, count, stride=groups), :] = product[count:, LANES:] + summary[s + 1]
    carried = jnp.zeros((groups, LANES), F32)
    scale = loads[...]
    for r in range(count):
        previous[r] = carried
        carried = rates[r] * carried + tiles[r * groups : (r + 1) * groups, :]
        value = (scale * carried).astype(BF16)
        for b in range(owners):
            reply[r * owners + b] = value


def residual_kernel(
    tile, phi, y, arrived, message, kept, phi_here, y_here, weights, total, spread, sems
):
    chunks = start_chunks(tile, ((y, y_here), (phi, phi_here)), sems)
    traits = arrived.shape[0]
    load_by_trait(arrived, spread, weights, 0)
    weights[traits:, :] = weights[:traits, :]
    kept[...] = weights[:traits, :]
    for i, (at, copies) in enumerate(chunks):
        wait_all(copies)
        fitted = contract_lanes(weights[...], phi_here[at, :])[:traits]
        residual = (fitted - y_here[at, :].T.astype(F32)).astype(BF16)
        product = jnp.dot(residual, phi_here[at, :], preferred_element_type=F32)
        if i == 0:
            total[...] = product
        else:
            total[...] += product
    store_by_trait(total[...], spread, message)


def backward_kernel(count, traits, message, pattern, previous, rates, loads, *refs):
    *pieces, reply, mixing, tiles, sems = refs
    copies = start_mixing(pieces, mixing, sems)
    devices = message.shape[0]
    owners = devices // count
    groups = mixing.shape[0] // LANES
    halves = groups // owners
    scale = loads[...]
    adjoint = jnp.zeros((groups, LANES), F32)
    for r in reversed(range(count)):
        pulled = message[r * owners].astype(F32)
        for b in range(1, owners):
            pulled = pulled + message[r * owners + b].astype(F32)
        pulled = scale * pulled
        if r + 1 < count:
            adjoint = pulled + rates[r + 1] * adjoint
        else:
            adjoint = pulled
        tiles[r * groups : (r + 1) * groups, :] = adjoint
        slope = adjoint * previous[r] * (1.0 / traits)
        high, low = split(slope)
        high, low = high.astype(F32), low.astype(F32)
        for b in range(owners):
            mine = slice(b * halves, (b + 1) * halves)
            tail = jnp.concatenate(
                [high[mine], low[mine], jnp.zeros((groups - 2 * halves, LANES), F32)], axis=0
            )
            reply[r * owners + b, groups : 2 * groups, :] = tail.astype(BF16)
    blocks = [
        tiles[pl.ds(s, count, stride=groups), :].astype(BF16).astype(F32) for s in range(groups)
    ]
    wait_all(copies)
    for s in range(0, groups, 2):
        kept = [keep(blocks, [pattern[k, t] for k in range(groups)]) for t in (s, s + 1)]
        product = jnp.dot(
            jnp.concatenate(kept, axis=0),
            mixing[:, s * LANES : (s + 2) * LANES],
            preferred_element_type=F32,
        )
        tiles[pl.ds(s, count, stride=groups), :] = product[:count, :LANES] + blocks[s]
        tiles[pl.ds(s + 1, count, stride=groups), :] = product[count:, LANES:] + blocks[s + 1]
    for r in range(count):
        back = tiles[r * groups : (r + 1) * groups, :].astype(BF16)
        for b in range(owners):
            reply[r * owners + b, 0:groups, :] = back


def gradient_kernel(
    tile,
    halves,
    phi,
    y,
    loaded,
    arrived,
    out,
    slope,
    phi_here,
    y_here,
    out_here,
    weights,
    spread,
    sems,
):
    chunks = start_chunks(tile, ((y, y_here), (phi, phi_here)), sems)
    traits = loaded.shape[0]
    groups = weights.shape[1] // LANES
    load_by_trait(arrived, spread, weights, 0)
    weights[traits:, :] = loaded[...]
    stores = []
    for i, (at, copies) in enumerate(chunks):
        wait_all(copies)
        both = contract_lanes(weights[...], phi_here[at, :])
        residual = (both[traits:] - y_here[at, :].T.astype(F32)).astype(BF16)
        out_here[at, :] = (both[:traits] - residual.astype(F32)).astype(BF16).T
        stores.append(pltpu.make_async_copy(out_here.at[at], out.at[at], sems.at[2, i]))
        stores[-1].start()
    tail = jnp.sum(arrived[:, groups : 2 * groups, :].astype(F32), axis=0)
    for h in range(halves):
        slope[:, h * LANES : (h + 1) * LANES] = (
            tail[h : h + 1, :] + tail[halves + h : halves + h + 1, :]
        )
    wait_all(stores)


def permute(value, target):
    pairs = []
    for r in range(lax.axis_size("region")):
        for b in range(OWNERS):
            to_r, to_b = target(r, b)
            pairs.append((r * OWNERS + b, to_r * OWNERS + to_b % OWNERS))
    return lax.ppermute(value, ALL, pairs)


def near_shard(mixing):
    return permute(mixing, lambda r, b: (r, b + 1 + 2 * (r % 2)))


def other_shards(near):
    swapped = permute(near, lambda r, b: (r ^ 1, b))
    across = permute(near, lambda r, b: (r ^ 1, b + 1 + 2 * (r % 2)))
    return swapped, across


def shards(count, observations, basis_values, mixing, pattern, decays, loadings):
    devices = lax.axis_size("region") * lax.axis_size("basis")
    rows, width = basis_values.shape
    traits = observations.shape[1]
    groups = width // LANES
    share = decays.shape[1]
    halves = share // LANES
    tile = min(TILE_ROWS, rows)
    chunks = rows // tile
    near = near_shard(mixing)

    hbm = pl.BlockSpec(memory_space=pl.ANY)
    vmem = pl.BlockSpec(memory_space=pltpu.VMEM)
    smem = pl.BlockSpec(memory_space=pltpu.SMEM)
    phi_here = pltpu.VMEM((rows, width), BF16)
    y_here = pltpu.VMEM((rows, traits), BF16)
    total = pltpu.VMEM((traits, width), F32)
    spread = pltpu.VMEM((traits * groups, LANES), F32)
    tiles = pltpu.VMEM((count * groups, LANES), F32)
    mixing_here = pltpu.VMEM((width, width), BF16)
    short = jax.ShapeDtypeStruct((devices, groups, LANES), BF16)
    long = jax.ShapeDtypeStruct((devices, 2 * groups, LANES), BF16)

    def sems(*shape):
        return pltpu.SemaphoreType.DMA(shape)

    def limit(mebibytes):
        return pltpu.CompilerParams(vmem_limit_bytes=mebibytes * MIB)

    def exchange(value):
        return lax.all_to_all(value, ALL, 0, 0, tiled=True)

    sums = pl.pallas_call(
        functools.partial(summary_kernel, tile),
        in_specs=[hbm] * 4,
        out_specs=vmem,
        out_shape=long,
        scratch_shapes=[
            phi_here,
            y_here,
            pltpu.VMEM((1, share), F32),
            pltpu.VMEM((1, share), F32),
            total,
            spread,
            sems(2, chunks),
            sems(2),
        ],
        compiler_params=limit(60),
        name="summary",
    )(basis_values, observations, decays, loadings[None, :])
    sums, near = lax.optimization_barrier((sums, near))
    pieces = (mixing, near) + other_shards(near)
    sums = exchange(sums)
    loaded, previous, rates, loads = pl.pallas_call(
        functools.partial(forward_kernel, count),
        in_specs=[vmem, smem] + [hbm] * len(pieces),
        out_specs=(vmem,) * 4,
        out_shape=(
            short,
            jax.ShapeDtypeStruct((count, groups, LANES), F32),
            jax.ShapeDtypeStruct((count, groups, LANES), F32),
            jax.ShapeDtypeStruct((groups, LANES), F32),
        ),
        scratch_shapes=[
            mixing_here,
            pltpu.VMEM((devices * 2 * groups, LANES), F32),
            tiles,
            sems(len(pieces)),
        ],
        compiler_params=limit(16),
        name="forward",
    )(sums, pattern, *pieces)
    loaded = exchange(loaded)
    pulled, loaded = pl.pallas_call(
        functools.partial(residual_kernel, tile),
        in_specs=[hbm, hbm, vmem],
        out_specs=(vmem, vmem),
        out_shape=(short, jax.ShapeDtypeStruct((traits, width), BF16)),
        scratch_shapes=[
            phi_here,
            y_here,
            pltpu.VMEM((2 * traits, width), BF16),
            total,
            spread,
            sems(2, chunks),
        ],
        compiler_params=limit(44),
        name="residual",
    )(basis_values, observations, loaded)
    pulled = exchange(pulled)
    back = pl.pallas_call(
        functools.partial(backward_kernel, count, traits),
        in_specs=[vmem, smem, vmem, vmem, vmem] + [hbm] * len(pieces),
        out_specs=vmem,
        out_shape=long,
        scratch_shapes=[mixing_here, tiles, sems(len(pieces))],
        compiler_params=limit(16),
        name="backward",
    )(pulled, pattern, previous, rates, loads, *pieces)
    back = exchange(back)
    obs_grad, slope = pl.pallas_call(
        functools.partial(gradient_kernel, tile, halves),
        in_specs=[hbm, hbm, vmem, vmem],
        out_specs=(hbm, vmem),
        out_shape=(
            jax.ShapeDtypeStruct((rows, traits), BF16),
            jax.ShapeDtypeStruct((1, share), F32),
        ),
        scratch_shapes=[
            phi_here,
            y_here,
            y_here,
            pltpu.VMEM((2 * traits, width), BF16),
            spread,
            sems(3, chunks),
        ],
        compiler_params=limit(44),
        name="gradient",
    )(basis_values, observations, loaded, back)
    return obs_grad, slope


def solution(mesh):
    in_specs = (
        P(ALL, None),
        P(ALL, None),
        P("basis", None),
        P(),
        P("region", "basis"),
        P("basis"),
    )
    out_specs = (P(ALL, None), P("region", "basis"))
    body = functools.partial(shards, mesh.shape["region"])
    return jax.shard_map(body, mesh=mesh, in_specs=in_specs, out_specs=out_specs, check_vma=False)
```

```python
import functools

import jax
import jax.numpy as jnp
from jax import lax
from jax.experimental import pallas as pl
from jax.experimental.pallas import tpu as pltpu
from jax.sharding import PartitionSpec as P

BLOCK = 128
LANES = 128
TILE_ROWS = 1024
MIB = 1024 * 1024
ALL = ("region", "basis")
F32 = jnp.float32
BF16 = jnp.bfloat16
OWNERS = 4
PART_ROWS = 4
PARTS = 3


def split(value):
    high = value.astype(BF16)
    return high, (value - high.astype(F32)).astype(BF16)


def start_chunks(sizes, pairs, sems):
    chunks = []
    start = 0
    for i, size in enumerate(sizes):
        at = pl.ds(start, size)
        start += size
        copies = [
            pltpu.make_async_copy(source.at[at], target.at[at], sems.at[k, i])
            for k, (source, target) in enumerate(pairs)
        ]
        for copy in copies:
            copy.start()
        chunks.append((at, copies))
    return chunks


def wait_all(copies):
    for copy in copies:
        copy.wait()


def piece_blocks():
    owner = lax.axis_index("basis")
    core = lax.rem(lax.axis_index("region"), 2)
    return [2 * lax.rem(owner + shift, OWNERS) for shift in (0, 3 + 2 * core, 1 + 2 * core, 2)]


def keep(blocks, present):
    return jnp.concatenate(
        [(block * flag.astype(F32)).astype(BF16) for block, flag in zip(blocks, present)], axis=1
    )


def contract_lanes(first, second):
    return lax.dot_general(first, second, (((1,), (1,)), ((), ())), preferred_element_type=F32)


def store_by_trait(total, spread, message):
    traits, width = total.shape
    groups = width // LANES
    for s in range(groups):
        spread[pl.ds(s, traits, stride=groups), :] = total[:, s * LANES : (s + 1) * LANES]
    message[:, 0:groups, :] = spread[...].reshape(traits, groups, LANES).astype(BF16)


def gather_traits(spread, target, traits, groups):
    for s in range(groups):
        target[0:traits, s * LANES : (s + 1) * LANES] = spread[
            pl.ds(s, traits, stride=groups), :
        ].astype(BF16)


def load_by_trait(message, spread, target):
    traits = message.shape[0]
    groups = target.shape[1] // LANES
    spread[...] = message[...].astype(F32).reshape(traits * groups, LANES)
    gather_traits(spread, target, traits, groups)


def summary_kernel(
    sizes,
    phi,
    y,
    rates_away,
    loads_away,
    message,
    phi_here,
    y_here,
    rates,
    loads,
    total,
    spread,
    sems,
    small_sems,
):
    small = (
        pltpu.make_async_copy(rates_away, rates, small_sems.at[0]),
        pltpu.make_async_copy(loads_away, loads, small_sems.at[1]),
    )
    chunks = start_chunks(sizes, ((y, y_here), (phi, phi_here)), sems)
    for copy in small:
        copy.start()
    for i, (at, copies) in enumerate(chunks):
        wait_all(copies)
        product = jnp.dot(y_here[at, :].T, phi_here[at, :], preferred_element_type=F32)
        if i == 0:
            total[...] = product
        else:
            total[...] += product
    store_by_trait(total[...], spread, message)
    wait_all(small)
    groups = total.shape[1] // LANES
    pieces = []
    for vector in (rates, loads):
        width = vector.shape[1] // LANES
        parts = [split(vector[:, h * LANES : (h + 1) * LANES]) for h in range(width)]
        pieces += [part[0] for part in parts] + [part[1] for part in parts]
    tail = jnp.concatenate([piece.astype(F32) for piece in pieces], axis=0).astype(BF16)
    message[:, groups : groups + tail.shape[0], :] = jnp.broadcast_to(
        tail[None], (message.shape[0],) + tail.shape
    )


def forward_kernel(count, message, pattern, *refs):
    *pieces, reply, previous, rates, loads, sums, wide, tiles = refs
    devices, rows, _ = message.shape
    owners = devices // count
    groups = pieces[0].shape[1] // LANES
    halves = groups // owners
    wide[...] = message[...].astype(F32).reshape(devices * rows, LANES)
    step = owners * rows

    def column(row):
        return wide[pl.ds(row, count, stride=step), :]

    summary = []
    for s in range(groups):
        block = column(s)
        for b in range(1, owners):
            block = block + column(b * rows + s)
        summary.append(block.astype(BF16).astype(F32))
        sums[s] = summary[s]
    for b in range(owners):
        for h in range(halves):
            at = b * rows + groups + h
            rates_block = column(at) + column(at + halves)
            tiles[pl.ds(b * halves + h, count, stride=groups), :] = rates_block
    rates[...] = tiles[...].reshape(count, groups, LANES)
    load_rows = []
    for b in range(owners):
        for h in range(halves):
            at = b * rows + groups + 2 * halves + h
            load_rows.append(wide[at : at + 1, :] + wide[at + halves : at + halves + 1, :])
    loads[...] = jnp.concatenate(load_rows, axis=0)
    for piece, s in zip(pieces, piece_blocks()):
        kept = [keep(summary, [pattern[t, k] for k in range(groups)]) for t in (s, s + 1)]
        product = contract_lanes(jnp.concatenate(kept, axis=0), piece[...])
        tiles[pl.ds(s, count, stride=groups), :] = product[:count, :LANES] + sums[s]
        tiles[pl.ds(s + 1, count, stride=groups), :] = product[count:, LANES:] + sums[s + 1]
    carried = jnp.zeros((groups, LANES), F32)
    scale = loads[...]
    for r in range(count):
        previous[r] = carried
        carried = rates[r] * carried + tiles[r * groups : (r + 1) * groups, :]
        value = (scale * carried).astype(BF16)
        for b in range(owners):
            reply[r * owners + b] = value


def residual_kernel(sizes, phi, y, arrived, message, kept, phi_here, weights, total, spread, sems):
    chunks = start_chunks(sizes, ((phi, phi_here),), sems)
    traits = arrived.shape[0]
    load_by_trait(arrived, spread, weights)
    weights[traits:, :] = weights[:traits, :]
    kept[...] = weights[:traits, :]
    for i, (at, copies) in enumerate(chunks):
        wait_all(copies)
        fitted = contract_lanes(weights[...], phi_here[at, :])[:traits]
        residual = (fitted - y[at, :].T.astype(F32)).astype(BF16)
        product = jnp.dot(residual, phi_here[at, :], preferred_element_type=F32)
        if i == 0:
            total[...] = product
        else:
            total[...] += product
    store_by_trait(total[...], spread, message)


def backward_kernel(count, traits, message, pattern, previous, rates, loads, *refs):
    *pieces, reply, tiles = refs
    devices = message.shape[0]
    owners = devices // count
    groups = pieces[0].shape[1] // LANES
    halves = groups // owners
    scale = loads[...]
    adjoint = jnp.zeros((groups, LANES), F32)
    for r in reversed(range(count)):
        pulled = message[r * owners].astype(F32)
        for b in range(1, owners):
            pulled = pulled + message[r * owners + b].astype(F32)
        pulled = scale * pulled
        if r + 1 < count:
            adjoint = pulled + rates[r + 1] * adjoint
        else:
            adjoint = pulled
        tiles[r * groups : (r + 1) * groups, :] = adjoint
        slope = adjoint * previous[r] * (1.0 / traits)
        high, low = split(slope)
        high, low = high.astype(F32), low.astype(F32)
        for b in range(owners):
            mine = slice(b * halves, (b + 1) * halves)
            tail = jnp.concatenate([high[mine], low[mine]], axis=0)
            reply[(r * owners + b) * PARTS + PARTS - 1] = tail.astype(BF16)
    def block(s):
        return tiles[pl.ds(s, count, stride=groups), :].astype(BF16).astype(F32)

    blocks = [block(s) for s in range(groups)]
    firsts = piece_blocks()
    parts = [(block(s), block(s + 1)) for s in firsts]
    for s in range(0, groups, 2):
        product = jnp.zeros((2 * count, 2 * LANES), F32)
        for piece, first, part in zip(pieces, firsts, parts):
            kept = [keep(part, (pattern[first, t], pattern[first + 1, t])) for t in (s, s + 1)]
            product += jnp.dot(
                jnp.concatenate(kept, axis=0),
                piece[:, s * LANES : (s + 2) * LANES],
                preferred_element_type=F32,
            )
        tiles[pl.ds(s, count, stride=groups), :] = product[:count, :LANES] + blocks[s]
        tiles[pl.ds(s + 1, count, stride=groups), :] = product[count:, LANES:] + blocks[s + 1]
    for r in range(count):
        for part in range(PARTS - 1):
            at = r * groups + part * PART_ROWS
            back = tiles[at : at + PART_ROWS, :].astype(BF16)
            for b in range(owners):
                reply[(r * owners + b) * PARTS + part] = back


def gradient_kernel(
    sizes, halves, phi, y, loaded, arrived, out, slope, phi_here, out_here, weights, spread, sent, sems
):
    chunks = start_chunks(sizes, ((phi, phi_here),), sems)
    traits = loaded.shape[0]
    groups = weights.shape[1] // LANES
    for k in range(traits):
        for part in range(PARTS - 1):
            at = k * groups + part * PART_ROWS
            spread[at : at + PART_ROWS, :] = arrived[k * PARTS + part].astype(F32)
    gather_traits(spread, weights, traits, groups)
    weights[traits:, :] = loaded[...]
    stores = []

    def finish(i):
        at = chunks[i][0]
        both = sent[i % 2, :, 0 : sizes[i]]
        residual = (both[traits:] - y[at, :].T.astype(F32)).astype(BF16)
        out_here[at, :] = (both[:traits] - residual.astype(F32)).astype(BF16).T
        stores.append(pltpu.make_async_copy(out_here.at[at], out.at[at], sems.at[1, i]))
        stores[-1].start()

    for i, (at, copies) in enumerate(chunks):
        wait_all(copies)
        sent[i % 2, :, 0 : sizes[i]] = contract_lanes(weights[...], phi_here[at, :])
        if i > 0:
            finish(i - 1)
    finish(len(chunks) - 1)
    tail = jnp.sum(arrived[pl.ds(PARTS - 1, traits, stride=PARTS)].astype(F32), axis=0)
    for h in range(halves):
        slope[:, h * LANES : (h + 1) * LANES] = (
            tail[h : h + 1, :] + tail[halves + h : halves + h + 1, :]
        )
    wait_all(stores)


def permute(value, target):
    pairs = []
    for r in range(lax.axis_size("region")):
        for b in range(OWNERS):
            to_r, to_b = target(r, b)
            pairs.append((r * OWNERS + b, to_r * OWNERS + to_b % OWNERS))
    return lax.ppermute(value, ALL, pairs)


def near_shard(mixing):
    return permute(mixing, lambda r, b: (r, b + 1 + 2 * (r % 2)))


def other_shards(near):
    swapped = permute(near, lambda r, b: (r ^ 1, b))
    across = permute(near, lambda r, b: (r ^ 1, b + 1 + 2 * (r % 2)))
    return swapped, across


def shards(count, observations, basis_values, mixing, pattern, decays, loadings):
    devices = lax.axis_size("region") * lax.axis_size("basis")
    rows, width = basis_values.shape
    traits = observations.shape[1]
    groups = width // LANES
    share = decays.shape[1]
    halves = share // LANES
    tile = min(TILE_ROWS, rows)
    even = (tile,) * (rows // tile)
    tapered = (tile // 2,) * 2 + even[2:] + (tile // 2,) * 2
    near = near_shard(mixing)

    hbm = pl.BlockSpec(memory_space=pl.ANY)
    vmem = pl.BlockSpec(memory_space=pltpu.VMEM)
    smem = pl.BlockSpec(memory_space=pltpu.SMEM)
    phi_here = pltpu.VMEM((rows, width), BF16)
    y_here = pltpu.VMEM((rows, traits), BF16)
    total = pltpu.VMEM((traits, width), F32)
    spread = pltpu.VMEM((traits * groups, LANES), F32)
    tiles = pltpu.VMEM((count * groups, LANES), F32)
    short = jax.ShapeDtypeStruct((devices, groups, LANES), BF16)
    long = jax.ShapeDtypeStruct((devices, 2 * groups, LANES), BF16)

    def sems(*shape):
        return pltpu.SemaphoreType.DMA(shape)

    def limit(mebibytes):
        return pltpu.CompilerParams(vmem_limit_bytes=mebibytes * MIB)

    def exchange(value):
        return lax.all_to_all(value, ALL, 0, 0, tiled=True)

    sums = pl.pallas_call(
        functools.partial(summary_kernel, tapered),
        in_specs=[hbm] * 4,
        out_specs=vmem,
        out_shape=long,
        scratch_shapes=[
            phi_here,
            y_here,
            pltpu.VMEM((1, share), F32),
            pltpu.VMEM((1, share), F32),
            total,
            spread,
            sems(2, len(tapered)),
            sems(2),
        ],
        compiler_params=limit(60),
        name="summary",
    )(basis_values, observations, decays, loadings[None, :])
    sums, near = lax.optimization_barrier((sums, near))
    pieces = (mixing, near) + other_shards(near)
    sums = exchange(sums)
    loaded, previous, rates, loads = pl.pallas_call(
        functools.partial(forward_kernel, count),
        in_specs=[vmem, smem] + [vmem] * len(pieces),
        out_specs=(vmem,) * 4,
        out_shape=(
            short,
            jax.ShapeDtypeStruct((count, groups, LANES), F32),
            jax.ShapeDtypeStruct((count, groups, LANES), F32),
            jax.ShapeDtypeStruct((groups, LANES), F32),
        ),
        scratch_shapes=[
            pltpu.VMEM((groups, count, LANES), F32),
            pltpu.VMEM((devices * 2 * groups, LANES), F32),
            tiles,
        ],
        compiler_params=limit(16),
        name="forward",
    )(sums, pattern, *pieces)
    loaded = exchange(loaded)
    pulled, loaded = pl.pallas_call(
        functools.partial(residual_kernel, even),
        in_specs=[hbm, vmem, vmem],
        out_specs=(vmem, vmem),
        out_shape=(short, jax.ShapeDtypeStruct((traits, width), BF16)),
        scratch_shapes=[
            phi_here,
            pltpu.VMEM((2 * traits, width), BF16),
            total,
            spread,
            sems(1, len(even)),
        ],
        compiler_params=limit(44),
        name="residual",
    )(basis_values, observations, loaded)
    pulled = exchange(pulled)
    back = pl.pallas_call(
        functools.partial(backward_kernel, count, traits),
        in_specs=[vmem, smem, vmem, vmem, vmem] + [vmem] * len(pieces),
        out_specs=vmem,
        out_shape=jax.ShapeDtypeStruct((devices * PARTS, PART_ROWS, LANES), BF16),
        scratch_shapes=[tiles],
        compiler_params=limit(16),
        name="backward",
    )(pulled, pattern, previous, rates, loads, *pieces)
    back = exchange(back)
    obs_grad, slope = pl.pallas_call(
        functools.partial(gradient_kernel, tapered, halves),
        in_specs=[hbm, vmem, vmem, vmem],
        out_specs=(hbm, vmem),
        out_shape=(
            jax.ShapeDtypeStruct((rows, traits), BF16),
            jax.ShapeDtypeStruct((1, share), F32),
        ),
        scratch_shapes=[
            phi_here,
            y_here,
            pltpu.VMEM((2 * traits, width), BF16),
            spread,
            pltpu.VMEM((2, 2 * traits, tile), F32),
            sems(2, len(tapered)),
        ],
        compiler_params=limit(44),
        name="gradient",
    )(basis_values, observations, loaded, back)
    return obs_grad, slope


def solution(mesh):
    in_specs = (
        P(ALL, None),
        P(ALL, None),
        P("basis", None),
        P(),
        P("region", "basis"),
        P("basis"),
    )
    out_specs = (P(ALL, None), P("region", "basis"))
    body = functools.partial(shards, mesh.shape["region"])
    return jax.shard_map(body, mesh=mesh, in_specs=in_specs, out_specs=out_specs, check_vma=False)
```

```python
import functools

import jax
import jax.numpy as jnp
from jax import lax
from jax.experimental import pallas as pl
from jax.experimental.pallas import tpu as pltpu
from jax.sharding import PartitionSpec as P

BLOCK = 128
LANES = 128
TILE_ROWS = 1024
MIB = 1024 * 1024
ALL = ("region", "basis")
F32 = jnp.float32
BF16 = jnp.bfloat16
OWNERS = 4
PART_ROWS = 4
PARTS = 3


def split(value):
    high = value.astype(BF16)
    return high, (value - high.astype(F32)).astype(BF16)


def start_chunks(sizes, pairs, sems):
    chunks = []
    start = 0
    for i, size in enumerate(sizes):
        at = pl.ds(start, size)
        start += size
        copies = [
            pltpu.make_async_copy(source.at[at], target.at[at], sems.at[k, i])
            for k, (source, target) in enumerate(pairs)
        ]
        for copy in copies:
            copy.start()
        chunks.append((at, copies))
    return chunks


def wait_all(copies):
    for copy in copies:
        copy.wait()


def piece_blocks():
    owner = lax.axis_index("basis")
    core = lax.rem(lax.axis_index("region"), 2)
    return [2 * lax.rem(owner + shift, OWNERS) for shift in (0, 3 + 2 * core, 1 + 2 * core, 2)]


def keep(blocks, present):
    return jnp.concatenate(
        [(block * flag.astype(F32)).astype(BF16) for block, flag in zip(blocks, present)], axis=1
    )


def contract_lanes(first, second):
    return lax.dot_general(first, second, (((1,), (1,)), ((), ())), preferred_element_type=F32)


def scatter_traits(total, spread):
    traits, width = total.shape
    groups = width // LANES
    for s in range(groups):
        spread[pl.ds(s, traits, stride=groups), :] = total[:, s * LANES : (s + 1) * LANES]


def store_by_trait(total, spread, message):
    scatter_traits(total, spread)
    message[...] = spread[...].reshape(message.shape).astype(BF16)


def gather_traits(spread, target, traits, groups):
    for s in range(groups):
        target[0:traits, s * LANES : (s + 1) * LANES] = spread[
            pl.ds(s, traits, stride=groups), :
        ].astype(BF16)


def load_by_trait(message, spread, target):
    traits = message.shape[0]
    groups = target.shape[1] // LANES
    spread[...] = message[...].astype(F32).reshape(traits * groups, LANES)
    gather_traits(spread, target, traits, groups)


def summary_kernel(
    sizes,
    phi,
    y,
    rates_away,
    loads_away,
    message,
    phi_here,
    y_here,
    rates,
    loads,
    total,
    spread,
    sems,
    small_sems,
):
    small = (
        pltpu.make_async_copy(rates_away, rates, small_sems.at[0]),
        pltpu.make_async_copy(loads_away, loads, small_sems.at[1]),
    )
    chunks = start_chunks(sizes, ((y, y_here), (phi, phi_here)), sems)
    for copy in small:
        copy.start()
    for i, (at, copies) in enumerate(chunks):
        wait_all(copies)
        product = jnp.dot(y_here[at, :].T, phi_here[at, :], preferred_element_type=F32)
        if i == 0:
            total[...] = product
        else:
            total[...] += product
    scatter_traits(total[...], spread)
    wait_all(small)
    traits, width = total.shape
    groups = width // LANES
    rows = [slice(h * LANES, (h + 1) * LANES) for h in range(rates.shape[1] // LANES)]
    highs, lows = zip(*[split(rates[:, at]) for at in rows])
    first = lax.axis_index("region") == 0
    lows = [jnp.where(first, loads[:, at], low.astype(F32)) for at, low in zip(rows, lows)]
    tail = jnp.concatenate([high.astype(F32) for high in highs] + lows, axis=0).astype(BF16)
    for k in range(traits):
        for part in range(PARTS - 1):
            at = k * groups + part * PART_ROWS
            message[k * PARTS + part] = spread[at : at + PART_ROWS, :].astype(BF16)
        message[k * PARTS + PARTS - 1] = tail


def forward_kernel(count, message, pattern, *refs):
    *pieces, reply, previous, rates, loads, sums, wide, tiles = refs
    rows = PARTS * PART_ROWS
    devices = message.shape[0] // PARTS
    owners = devices // count
    groups = pieces[0].shape[1] // LANES
    halves = groups // owners
    for i in range(devices * PARTS):
        wide[i * PART_ROWS : (i + 1) * PART_ROWS, :] = message[i].astype(F32)
    step = owners * rows

    def column(row):
        return wide[pl.ds(row, count, stride=step), :]

    summary = []
    for s in range(groups):
        block = column(s)
        for b in range(1, owners):
            block = block + column(b * rows + s)
        summary.append(block.astype(BF16).astype(F32))
        sums[s] = summary[s]
    later = lax.broadcasted_iota(jnp.int32, (count, LANES), 0) > 0
    load_rows = []
    for b in range(owners):
        for h in range(halves):
            at = b * rows + groups + h
            low = jnp.where(later, column(at + halves), 0.0)
            tiles[pl.ds(b * halves + h, count, stride=groups), :] = column(at) + low
            load_rows.append(wide[at + halves : at + halves + 1, :])
    rates[...] = tiles[...].reshape(count, groups, LANES)
    loads[...] = jnp.concatenate(load_rows, axis=0)
    for piece, s in zip(pieces, piece_blocks()):
        kept = [keep(summary, [pattern[t, k] for k in range(groups)]) for t in (s, s + 1)]
        product = contract_lanes(jnp.concatenate(kept, axis=0), piece[...])
        tiles[pl.ds(s, count, stride=groups), :] = product[:count, :LANES] + sums[s]
        tiles[pl.ds(s + 1, count, stride=groups), :] = product[count:, LANES:] + sums[s + 1]
    carried = jnp.zeros((groups, LANES), F32)
    scale = loads[...]
    for r in range(count):
        previous[r] = carried
        carried = rates[r] * carried + tiles[r * groups : (r + 1) * groups, :]
        value = (scale * carried).astype(BF16)
        for b in range(owners):
            reply[r * owners + b] = value


def residual_kernel(sizes, phi, y, arrived, message, kept, phi_here, weights, total, spread, sems):
    chunks = start_chunks(sizes, ((phi, phi_here),), sems)
    traits = arrived.shape[0]
    load_by_trait(arrived, spread, weights)
    weights[traits:, :] = weights[:traits, :]
    kept[...] = weights[:traits, :]
    for i, (at, copies) in enumerate(chunks):
        wait_all(copies)
        fitted = contract_lanes(weights[...], phi_here[at, :])[:traits]
        residual = (fitted - y[at, :].T.astype(F32)).astype(BF16)
        product = jnp.dot(residual, phi_here[at, :], preferred_element_type=F32)
        if i == 0:
            total[...] = product
        else:
            total[...] += product
    store_by_trait(total[...], spread, message)


def backward_kernel(count, traits, message, pattern, previous, rates, loads, *refs):
    *pieces, reply, tiles = refs
    devices = message.shape[0]
    owners = devices // count
    groups = pieces[0].shape[1] // LANES
    halves = groups // owners
    scale = loads[...]
    adjoint = jnp.zeros((groups, LANES), F32)
    for r in reversed(range(count)):
        pulled = message[r * owners].astype(F32)
        for b in range(1, owners):
            pulled = pulled + message[r * owners + b].astype(F32)
        pulled = scale * pulled
        if r + 1 < count:
            adjoint = pulled + rates[r + 1] * adjoint
        else:
            adjoint = pulled
        tiles[r * groups : (r + 1) * groups, :] = adjoint
        slope = adjoint * previous[r] * (1.0 / traits)
        high, low = split(slope)
        high, low = high.astype(F32), low.astype(F32)
        for b in range(owners):
            mine = slice(b * halves, (b + 1) * halves)
            tail = jnp.concatenate([high[mine], low[mine]], axis=0)
            reply[(r * owners + b) * PARTS + PARTS - 1] = tail.astype(BF16)
    def block(s):
        return tiles[pl.ds(s, count, stride=groups), :].astype(BF16).astype(F32)

    blocks = [block(s) for s in range(groups)]
    firsts = piece_blocks()
    parts = [(block(s), block(s + 1)) for s in firsts]
    for s in range(0, groups, 2):
        product = jnp.zeros((2 * count, 2 * LANES), F32)
        for piece, first, part in zip(pieces, firsts, parts):
            kept = [keep(part, (pattern[first, t], pattern[first + 1, t])) for t in (s, s + 1)]
            product += jnp.dot(
                jnp.concatenate(kept, axis=0),
                piece[:, s * LANES : (s + 2) * LANES],
                preferred_element_type=F32,
            )
        tiles[pl.ds(s, count, stride=groups), :] = product[:count, :LANES] + blocks[s]
        tiles[pl.ds(s + 1, count, stride=groups), :] = product[count:, LANES:] + blocks[s + 1]
    for r in range(count):
        for part in range(PARTS - 1):
            at = r * groups + part * PART_ROWS
            back = tiles[at : at + PART_ROWS, :].astype(BF16)
            for b in range(owners):
                reply[(r * owners + b) * PARTS + part] = back


def gradient_kernel(
    sizes, halves, phi, y, loaded, arrived, out, slope, phi_here, out_here, weights, spread, sent, sems
):
    chunks = start_chunks(sizes, ((phi, phi_here),), sems)
    traits = loaded.shape[0]
    groups = weights.shape[1] // LANES
    for k in range(traits):
        for part in range(PARTS - 1):
            at = k * groups + part * PART_ROWS
            spread[at : at + PART_ROWS, :] = arrived[k * PARTS + part].astype(F32)
    gather_traits(spread, weights, traits, groups)
    weights[traits:, :] = loaded[...]
    stores = []

    def finish(i):
        at = chunks[i][0]
        both = sent[i % 2, :, 0 : sizes[i]]
        residual = (both[traits:] - y[at, :].T.astype(F32)).astype(BF16)
        out_here[at, :] = (both[:traits] - residual.astype(F32)).astype(BF16).T
        stores.append(pltpu.make_async_copy(out_here.at[at], out.at[at], sems.at[1, i]))
        stores[-1].start()

    for i, (at, copies) in enumerate(chunks):
        wait_all(copies)
        sent[i % 2, :, 0 : sizes[i]] = contract_lanes(weights[...], phi_here[at, :])
        if i > 0:
            finish(i - 1)
    finish(len(chunks) - 1)
    tail = jnp.sum(arrived[pl.ds(PARTS - 1, traits, stride=PARTS)].astype(F32), axis=0)
    for h in range(halves):
        slope[:, h * LANES : (h + 1) * LANES] = (
            tail[h : h + 1, :] + tail[halves + h : halves + h + 1, :]
        )
    wait_all(stores)


def permute(value, target):
    pairs = []
    for r in range(lax.axis_size("region")):
        for b in range(OWNERS):
            to_r, to_b = target(r, b)
            pairs.append((r * OWNERS + b, to_r * OWNERS + to_b % OWNERS))
    return lax.ppermute(value, ALL, pairs)


def near_shard(mixing):
    return permute(mixing, lambda r, b: (r, b + 1 + 2 * (r % 2)))


def other_shards(near):
    swapped = permute(near, lambda r, b: (r ^ 1, b))
    across = permute(near, lambda r, b: (r ^ 1, b + 1 + 2 * (r % 2)))
    return swapped, across


def shards(count, observations, basis_values, mixing, pattern, decays, loadings):
    devices = lax.axis_size("region") * lax.axis_size("basis")
    rows, width = basis_values.shape
    traits = observations.shape[1]
    groups = width // LANES
    share = decays.shape[1]
    halves = share // LANES
    tile = min(TILE_ROWS, rows)
    even = (tile,) * (rows // tile)
    tapered = (tile // 2,) * 2 + even[2:] + (tile // 2,) * 2
    near = near_shard(mixing)

    hbm = pl.BlockSpec(memory_space=pl.ANY)
    vmem = pl.BlockSpec(memory_space=pltpu.VMEM)
    smem = pl.BlockSpec(memory_space=pltpu.SMEM)
    phi_here = pltpu.VMEM((rows, width), BF16)
    y_here = pltpu.VMEM((rows, traits), BF16)
    total = pltpu.VMEM((traits, width), F32)
    spread = pltpu.VMEM((traits * groups, LANES), F32)
    tiles = pltpu.VMEM((count * groups, LANES), F32)
    short = jax.ShapeDtypeStruct((devices, groups, LANES), BF16)
    long = jax.ShapeDtypeStruct((devices * PARTS, PART_ROWS, LANES), BF16)

    def sems(*shape):
        return pltpu.SemaphoreType.DMA(shape)

    def limit(mebibytes):
        return pltpu.CompilerParams(vmem_limit_bytes=mebibytes * MIB)

    def exchange(value):
        return lax.all_to_all(value, ALL, 0, 0, tiled=True)

    sums = pl.pallas_call(
        functools.partial(summary_kernel, tapered),
        in_specs=[hbm] * 4,
        out_specs=vmem,
        out_shape=long,
        scratch_shapes=[
            phi_here,
            y_here,
            pltpu.VMEM((1, share), F32),
            pltpu.VMEM((1, share), F32),
            total,
            spread,
            sems(2, len(tapered)),
            sems(2),
        ],
        compiler_params=limit(60),
        name="summary",
    )(basis_values, observations, decays, loadings[None, :])
    sums, near = lax.optimization_barrier((sums, near))
    pieces = (mixing, near) + other_shards(near)
    sums = exchange(sums)
    loaded, previous, rates, loads = pl.pallas_call(
        functools.partial(forward_kernel, count),
        in_specs=[vmem, smem] + [vmem] * len(pieces),
        out_specs=(vmem,) * 4,
        out_shape=(
            short,
            jax.ShapeDtypeStruct((count, groups, LANES), F32),
            jax.ShapeDtypeStruct((count, groups, LANES), F32),
            jax.ShapeDtypeStruct((groups, LANES), F32),
        ),
        scratch_shapes=[
            pltpu.VMEM((groups, count, LANES), F32),
            pltpu.VMEM((devices * PARTS * PART_ROWS, LANES), F32),
            tiles,
        ],
        compiler_params=limit(16),
        name="forward",
    )(sums, pattern, *pieces)
    loaded = exchange(loaded)
    pulled, loaded = pl.pallas_call(
        functools.partial(residual_kernel, even),
        in_specs=[hbm, vmem, vmem],
        out_specs=(vmem, vmem),
        out_shape=(short, jax.ShapeDtypeStruct((traits, width), BF16)),
        scratch_shapes=[
            phi_here,
            pltpu.VMEM((2 * traits, width), BF16),
            total,
            spread,
            sems(1, len(even)),
        ],
        compiler_params=limit(44),
        name="residual",
    )(basis_values, observations, loaded)
    pulled = exchange(pulled)
    back = pl.pallas_call(
        functools.partial(backward_kernel, count, traits),
        in_specs=[vmem, smem, vmem, vmem, vmem] + [vmem] * len(pieces),
        out_specs=vmem,
        out_shape=long,
        scratch_shapes=[tiles],
        compiler_params=limit(16),
        name="backward",
    )(pulled, pattern, previous, rates, loads, *pieces)
    back = exchange(back)
    obs_grad, slope = pl.pallas_call(
        functools.partial(gradient_kernel, tapered, halves),
        in_specs=[hbm, vmem, vmem, vmem],
        out_specs=(hbm, vmem),
        out_shape=(
            jax.ShapeDtypeStruct((rows, traits), BF16),
            jax.ShapeDtypeStruct((1, share), F32),
        ),
        scratch_shapes=[
            phi_here,
            y_here,
            pltpu.VMEM((2 * traits, width), BF16),
            spread,
            pltpu.VMEM((2, 2 * traits, tile), F32),
            sems(2, len(tapered)),
        ],
        compiler_params=limit(44),
        name="gradient",
    )(basis_values, observations, loaded, back)
    return obs_grad, slope


def solution(mesh):
    in_specs = (
        P(ALL, None),
        P(ALL, None),
        P("basis", None),
        P(),
        P("region", "basis"),
        P("basis"),
    )
    out_specs = (P(ALL, None), P("region", "basis"))
    body = functools.partial(shards, mesh.shape["region"])
    return jax.shard_map(body, mesh=mesh, in_specs=in_specs, out_specs=out_specs, check_vma=False)
```

```python
import functools

import jax
import jax.numpy as jnp
from jax import lax
from jax.experimental import pallas as pl
from jax.experimental.pallas import tpu as pltpu
from jax.sharding import PartitionSpec as P

BLOCK = 128
LANES = 128
TILE_ROWS = 1024
MIB = 1024 * 1024
ALL = ("region", "basis")
F32 = jnp.float32
BF16 = jnp.bfloat16
OWNERS = 4
PART_ROWS = 4
PARTS = 3


def split(value):
    high = value.astype(BF16)
    return high, (value - high.astype(F32)).astype(BF16)


def start_chunks(sizes, pairs, sems):
    chunks = []
    start = 0
    for i, size in enumerate(sizes):
        at = pl.ds(start, size)
        start += size
        copies = [
            pltpu.make_async_copy(source.at[at], target.at[at], sems.at[k, i])
            for k, (source, target) in enumerate(pairs)
        ]
        for copy in copies:
            copy.start()
        chunks.append((at, copies))
    return chunks


def wait_all(copies):
    for copy in copies:
        copy.wait()


def piece_blocks():
    owner = lax.axis_index("basis")
    core = lax.rem(lax.axis_index("region"), 2)
    return [2 * lax.rem(owner + shift, OWNERS) for shift in (0, 3 + 2 * core, 1 + 2 * core, 2)]


def keep(blocks, present):
    return jnp.concatenate(
        [(block * flag.astype(F32)).astype(BF16) for block, flag in zip(blocks, present)], axis=1
    )


def contract_lanes(first, second):
    return lax.dot_general(first, second, (((1,), (1,)), ((), ())), preferred_element_type=F32)


def scatter_traits(total, spread):
    traits, width = total.shape
    groups = width // LANES
    for s in range(groups):
        spread[pl.ds(s, traits, stride=groups), :] = total[:, s * LANES : (s + 1) * LANES]


def store_by_trait(total, spread, message):
    scatter_traits(total, spread)
    message[...] = spread[...].reshape(message.shape).astype(BF16)


def gather_traits(spread, target, traits, groups):
    for s in range(groups):
        target[0:traits, s * LANES : (s + 1) * LANES] = spread[
            pl.ds(s, traits, stride=groups), :
        ].astype(BF16)


def load_by_trait(message, spread, target):
    traits = message.shape[0]
    groups = target.shape[1] // LANES
    spread[...] = message[...].astype(F32).reshape(traits * groups, LANES)
    gather_traits(spread, target, traits, groups)


def summary_kernel(
    sizes,
    phi,
    y,
    rates_away,
    loads_away,
    message,
    phi_here,
    y_here,
    rates,
    loads,
    total,
    spread,
    sems,
    small_sems,
):
    small = (
        pltpu.make_async_copy(rates_away, rates, small_sems.at[0]),
        pltpu.make_async_copy(loads_away, loads, small_sems.at[1]),
    )
    chunks = start_chunks(sizes, ((y, y_here), (phi, phi_here)), sems)
    for copy in small:
        copy.start()
    for i, (at, copies) in enumerate(chunks):
        wait_all(copies)
        product = jnp.dot(y_here[at, :].T, phi_here[at, :], preferred_element_type=F32)
        if i == 0:
            total[...] = product
        else:
            total[...] += product
    scatter_traits(total[...], spread)
    wait_all(small)
    traits, width = total.shape
    groups = width // LANES
    rows = [slice(h * LANES, (h + 1) * LANES) for h in range(rates.shape[1] // LANES)]
    highs, lows = zip(*[split(rates[:, at]) for at in rows])
    first = lax.axis_index("region") == 0
    lows = [jnp.where(first, loads[:, at], low.astype(F32)) for at, low in zip(rows, lows)]
    tail = jnp.concatenate([high.astype(F32) for high in highs] + lows, axis=0).astype(BF16)
    for k in range(traits):
        for part in range(PARTS - 1):
            at = k * groups + part * PART_ROWS
            message[k * PARTS + part] = spread[at : at + PART_ROWS, :].astype(BF16)
        message[k * PARTS + PARTS - 1] = tail


def forward_kernel(count, message, pattern, *refs):
    *pieces, reply, previous, rates, loads, sums, wide, tiles = refs
    rows = PARTS * PART_ROWS
    devices = message.shape[0] // PARTS
    owners = devices // count
    groups = pieces[0].shape[1] // LANES
    halves = groups // owners
    for i in range(devices * PARTS):
        wide[i * PART_ROWS : (i + 1) * PART_ROWS, :] = message[i].astype(F32)
    step = owners * rows

    def column(row):
        return wide[pl.ds(row, count, stride=step), :]

    summary = []
    for s in range(groups):
        block = column(s)
        for b in range(1, owners):
            block = block + column(b * rows + s)
        summary.append(block.astype(BF16).astype(F32))
        sums[s] = summary[s]
    later = lax.broadcasted_iota(jnp.int32, (count, LANES), 0) > 0
    load_rows = []
    for b in range(owners):
        for h in range(halves):
            at = b * rows + groups + h
            low = jnp.where(later, column(at + halves), 0.0)
            tiles[pl.ds(b * halves + h, count, stride=groups), :] = column(at) + low
            load_rows.append(wide[at + halves : at + halves + 1, :])
    rates[...] = tiles[...].reshape(count, groups, LANES)
    loads[...] = jnp.concatenate(load_rows, axis=0)
    for piece, s in zip(pieces, piece_blocks()):
        kept = [keep(summary, [pattern[t, k] for k in range(groups)]) for t in (s, s + 1)]
        product = contract_lanes(jnp.concatenate(kept, axis=0), piece[...])
        tiles[pl.ds(s, count, stride=groups), :] = product[:count, :LANES] + sums[s]
        tiles[pl.ds(s + 1, count, stride=groups), :] = product[count:, LANES:] + sums[s + 1]
    carried = jnp.zeros((groups, LANES), F32)
    scale = loads[...]
    for r in range(count):
        previous[r] = carried
        carried = rates[r] * carried + tiles[r * groups : (r + 1) * groups, :]
        value = (scale * carried).astype(BF16)
        for b in range(owners):
            reply[r * owners + b] = value


def residual_kernel(
    sizes, phi, y, arrived, message, residuals, phi_here, weights, total, spread, sems
):
    chunks = start_chunks(sizes, ((phi, phi_here),), sems)
    traits = arrived.shape[0]
    load_by_trait(arrived, spread, weights)
    weights[traits:, :] = weights[:traits, :]
    for i, (at, copies) in enumerate(chunks):
        wait_all(copies)
        fitted = contract_lanes(weights[...], phi_here[at, :])[:traits]
        residual = (fitted - y[at, :].T.astype(F32)).astype(BF16)
        residuals[:, at] = residual
        product = jnp.dot(residual, phi_here[at, :], preferred_element_type=F32)
        if i == 0:
            total[...] = product
        else:
            total[...] += product
    store_by_trait(total[...], spread, message)


def backward_kernel(count, traits, message, pattern, previous, rates, loads, *refs):
    *pieces, reply, tiles = refs
    devices = message.shape[0]
    owners = devices // count
    groups = pieces[0].shape[1] // LANES
    halves = groups // owners
    scale = loads[...]
    adjoint = jnp.zeros((groups, LANES), F32)
    for r in reversed(range(count)):
        pulled = message[r * owners].astype(F32)
        for b in range(1, owners):
            pulled = pulled + message[r * owners + b].astype(F32)
        pulled = scale * pulled
        if r + 1 < count:
            adjoint = pulled + rates[r + 1] * adjoint
        else:
            adjoint = pulled
        tiles[r * groups : (r + 1) * groups, :] = adjoint
        slope = adjoint * previous[r] * (1.0 / traits)
        high, low = split(slope)
        high, low = high.astype(F32), low.astype(F32)
        for b in range(owners):
            mine = slice(b * halves, (b + 1) * halves)
            tail = jnp.concatenate([high[mine], low[mine]], axis=0)
            reply[(r * owners + b) * PARTS + PARTS - 1] = tail.astype(BF16)
    def block(s):
        return tiles[pl.ds(s, count, stride=groups), :].astype(BF16).astype(F32)

    blocks = [block(s) for s in range(groups)]
    firsts = piece_blocks()
    parts = [(block(s), block(s + 1)) for s in firsts]
    for s in range(0, groups, 2):
        product = jnp.zeros((2 * count, 2 * LANES), F32)
        for piece, first, part in zip(pieces, firsts, parts):
            kept = [keep(part, (pattern[first, t], pattern[first + 1, t])) for t in (s, s + 1)]
            product += jnp.dot(
                jnp.concatenate(kept, axis=0),
                piece[:, s * LANES : (s + 2) * LANES],
                preferred_element_type=F32,
            )
        tiles[pl.ds(s, count, stride=groups), :] = product[:count, :LANES] + blocks[s]
        tiles[pl.ds(s + 1, count, stride=groups), :] = product[count:, LANES:] + blocks[s + 1]
    for r in range(count):
        for part in range(PARTS - 1):
            at = r * groups + part * PART_ROWS
            back = tiles[at : at + PART_ROWS, :].astype(BF16)
            for b in range(owners):
                reply[(r * owners + b) * PARTS + part] = back


def gradient_kernel(
    sizes, halves, phi, residuals, arrived, out, slope, phi_here, out_here, weights, spread, sent, sems
):
    chunks = start_chunks(sizes, ((phi, phi_here),), sems)
    traits = residuals.shape[0]
    groups = weights.shape[1] // LANES
    for k in range(traits):
        for part in range(PARTS - 1):
            at = k * groups + part * PART_ROWS
            spread[at : at + PART_ROWS, :] = arrived[k * PARTS + part].astype(F32)
    gather_traits(spread, weights, traits, groups)
    weights[traits:, :] = weights[:traits, :]
    stores = []

    def finish(i):
        at = chunks[i][0]
        back = sent[i % 2, :, 0 : sizes[i]]
        out_here[at, :] = (back - residuals[:, at].astype(F32)).astype(BF16).T
        stores.append(pltpu.make_async_copy(out_here.at[at], out.at[at], sems.at[1, i]))
        stores[-1].start()

    for i, (at, copies) in enumerate(chunks):
        wait_all(copies)
        sent[i % 2, :, 0 : sizes[i]] = contract_lanes(weights[...], phi_here[at, :])[:traits]
        if i > 0:
            finish(i - 1)
    finish(len(chunks) - 1)
    tail = jnp.sum(arrived[pl.ds(PARTS - 1, traits, stride=PARTS)].astype(F32), axis=0)
    for h in range(halves):
        slope[:, h * LANES : (h + 1) * LANES] = (
            tail[h : h + 1, :] + tail[halves + h : halves + h + 1, :]
        )
    wait_all(stores)


def permute(value, target):
    pairs = []
    for r in range(lax.axis_size("region")):
        for b in range(OWNERS):
            to_r, to_b = target(r, b)
            pairs.append((r * OWNERS + b, to_r * OWNERS + to_b % OWNERS))
    return lax.ppermute(value, ALL, pairs)


def near_shard(mixing):
    return permute(mixing, lambda r, b: (r, b + 1 + 2 * (r % 2)))


def other_shards(near):
    swapped = permute(near, lambda r, b: (r ^ 1, b))
    across = permute(near, lambda r, b: (r ^ 1, b + 1 + 2 * (r % 2)))
    return swapped, across


def shards(count, observations, basis_values, mixing, pattern, decays, loadings):
    devices = lax.axis_size("region") * lax.axis_size("basis")
    rows, width = basis_values.shape
    traits = observations.shape[1]
    groups = width // LANES
    share = decays.shape[1]
    halves = share // LANES
    tile = min(TILE_ROWS, rows)
    even = (tile,) * (rows // tile)
    tapered = (tile // 2,) * 2 + even[2:] + (tile // 2, tile // 4, tile // 4)
    near = near_shard(mixing)

    hbm = pl.BlockSpec(memory_space=pl.ANY)
    vmem = pl.BlockSpec(memory_space=pltpu.VMEM)
    smem = pl.BlockSpec(memory_space=pltpu.SMEM)
    phi_here = pltpu.VMEM((rows, width), BF16)
    y_here = pltpu.VMEM((rows, traits), BF16)
    total = pltpu.VMEM((traits, width), F32)
    spread = pltpu.VMEM((traits * groups, LANES), F32)
    tiles = pltpu.VMEM((count * groups, LANES), F32)
    short = jax.ShapeDtypeStruct((devices, groups, LANES), BF16)
    long = jax.ShapeDtypeStruct((devices * PARTS, PART_ROWS, LANES), BF16)

    def sems(*shape):
        return pltpu.SemaphoreType.DMA(shape)

    def limit(mebibytes):
        return pltpu.CompilerParams(vmem_limit_bytes=mebibytes * MIB)

    def exchange(value):
        return lax.all_to_all(value, ALL, 0, 0, tiled=True)

    sums = pl.pallas_call(
        functools.partial(summary_kernel, tapered),
        in_specs=[hbm] * 4,
        out_specs=vmem,
        out_shape=long,
        scratch_shapes=[
            phi_here,
            y_here,
            pltpu.VMEM((1, share), F32),
            pltpu.VMEM((1, share), F32),
            total,
            spread,
            sems(2, len(tapered)),
            sems(2),
        ],
        compiler_params=limit(60),
        name="summary",
    )(basis_values, observations, decays, loadings[None, :])
    sums, near = lax.optimization_barrier((sums, near))
    pieces = (mixing, near) + other_shards(near)
    sums = exchange(sums)
    loaded, previous, rates, loads = pl.pallas_call(
        functools.partial(forward_kernel, count),
        in_specs=[vmem, smem] + [vmem] * len(pieces),
        out_specs=(vmem,) * 4,
        out_shape=(
            short,
            jax.ShapeDtypeStruct((count, groups, LANES), F32),
            jax.ShapeDtypeStruct((count, groups, LANES), F32),
            jax.ShapeDtypeStruct((groups, LANES), F32),
        ),
        scratch_shapes=[
            pltpu.VMEM((groups, count, LANES), F32),
            pltpu.VMEM((devices * PARTS * PART_ROWS, LANES), F32),
            tiles,
        ],
        compiler_params=limit(16),
        name="forward",
    )(sums, pattern, *pieces)
    loaded = exchange(loaded)
    pulled, residuals = pl.pallas_call(
        functools.partial(residual_kernel, even),
        in_specs=[hbm, vmem, vmem],
        out_specs=(vmem, vmem),
        out_shape=(short, jax.ShapeDtypeStruct((traits, rows), BF16)),
        scratch_shapes=[
            phi_here,
            pltpu.VMEM((2 * traits, width), BF16),
            total,
            spread,
            sems(1, len(even)),
        ],
        compiler_params=limit(44),
        name="residual",
    )(basis_values, observations, loaded)
    pulled = exchange(pulled)
    back = pl.pallas_call(
        functools.partial(backward_kernel, count, traits),
        in_specs=[vmem, smem, vmem, vmem, vmem] + [vmem] * len(pieces),
        out_specs=vmem,
        out_shape=long,
        scratch_shapes=[tiles],
        compiler_params=limit(16),
        name="backward",
    )(pulled, pattern, previous, rates, loads, *pieces)
    back = exchange(back)
    obs_grad, slope = pl.pallas_call(
        functools.partial(gradient_kernel, tapered, halves),
        in_specs=[hbm, vmem, vmem],
        out_specs=(hbm, vmem),
        out_shape=(
            jax.ShapeDtypeStruct((rows, traits), BF16),
            jax.ShapeDtypeStruct((1, share), F32),
        ),
        scratch_shapes=[
            phi_here,
            y_here,
            pltpu.VMEM((2 * traits, width), BF16),
            spread,
            pltpu.VMEM((2, traits, tile), F32),
            sems(2, len(tapered)),
        ],
        compiler_params=limit(44),
        name="gradient",
    )(basis_values, residuals, back)
    return obs_grad, slope


def solution(mesh):
    in_specs = (
        P(ALL, None),
        P(ALL, None),
        P("basis", None),
        P(),
        P("region", "basis"),
        P("basis"),
    )
    out_specs = (P(ALL, None), P("region", "basis"))
    body = functools.partial(shards, mesh.shape["region"])
    return jax.shard_map(body, mesh=mesh, in_specs=in_specs, out_specs=out_specs, check_vma=False)
```

```python
import functools

import jax
import jax.numpy as jnp
from jax import lax
from jax.experimental import pallas as pl
from jax.experimental.pallas import tpu as pltpu
from jax.sharding import PartitionSpec as P

BLOCK = 128
LANES = 128
TILE_ROWS = 1024
MIB = 1024 * 1024
ALL = ("region", "basis")
F32 = jnp.float32
BF16 = jnp.bfloat16
OWNERS = 4
PART_ROWS = 4
PARTS = 3


def split(value):
    high = value.astype(BF16)
    return high, (value - high.astype(F32)).astype(BF16)


def start_chunks(sizes, pairs, sems):
    chunks = []
    start = 0
    for i, size in enumerate(sizes):
        at = pl.ds(start, size)
        start += size
        copies = [
            pltpu.make_async_copy(source.at[at], target.at[at], sems.at[k, i])
            for k, (source, target) in enumerate(pairs)
        ]
        for copy in copies:
            copy.start()
        chunks.append((at, copies))
    return chunks


def wait_all(copies):
    for copy in copies:
        copy.wait()


def piece_blocks():
    owner = lax.axis_index("basis")
    core = lax.rem(lax.axis_index("region"), 2)
    return [2 * lax.rem(owner + shift, OWNERS) for shift in (0, 3 + 2 * core, 1 + 2 * core, 2)]


def keep(blocks, present):
    return jnp.concatenate(
        [(block * flag.astype(F32)).astype(BF16) for block, flag in zip(blocks, present)], axis=1
    )


def contract_lanes(first, second):
    return lax.dot_general(first, second, (((1,), (1,)), ((), ())), preferred_element_type=F32)


def scatter_traits(total, spread):
    traits, width = total.shape
    groups = width // LANES
    for s in range(groups):
        spread[pl.ds(s, traits, stride=groups), :] = total[:, s * LANES : (s + 1) * LANES]


def store_by_trait(total, spread, message):
    scatter_traits(total, spread)
    message[...] = spread[...].reshape(message.shape).astype(BF16)


def gather_traits(spread, target, traits, groups):
    for s in range(groups):
        target[0:traits, s * LANES : (s + 1) * LANES] = spread[
            pl.ds(s, traits, stride=groups), :
        ].astype(BF16)


def load_by_trait(message, spread, target):
    traits = message.shape[0]
    groups = target.shape[1] // LANES
    spread[...] = message[...].astype(F32).reshape(traits * groups, LANES)
    gather_traits(spread, target, traits, groups)


def summary_kernel(
    sizes,
    phi,
    y,
    rates_away,
    loads_away,
    message,
    phi_here,
    y_here,
    rates,
    loads,
    total,
    spread,
    sems,
    small_sems,
):
    small = (
        pltpu.make_async_copy(rates_away, rates, small_sems.at[0]),
        pltpu.make_async_copy(loads_away, loads, small_sems.at[1]),
    )
    chunks = start_chunks(sizes, ((y, y_here), (phi, phi_here)), sems)
    for copy in small:
        copy.start()
    for i, (at, copies) in enumerate(chunks):
        wait_all(copies)
        product = jnp.dot(y_here[at, :].T, phi_here[at, :], preferred_element_type=F32)
        if i == 0:
            total[...] = product
        else:
            total[...] += product
    scatter_traits(total[...], spread)
    wait_all(small)
    traits, width = total.shape
    groups = width // LANES
    rows = [slice(h * LANES, (h + 1) * LANES) for h in range(rates.shape[1] // LANES)]
    highs, lows = zip(*[split(rates[:, at]) for at in rows])
    first = lax.axis_index("region") == 0
    lows = [jnp.where(first, loads[:, at], low.astype(F32)) for at, low in zip(rows, lows)]
    tail = jnp.concatenate([high.astype(F32) for high in highs] + lows, axis=0).astype(BF16)
    for k in range(traits):
        for part in range(PARTS - 1):
            at = k * groups + part * PART_ROWS
            message[k * PARTS + part] = spread[at : at + PART_ROWS, :].astype(BF16)
        message[k * PARTS + PARTS - 1] = tail


def forward_kernel(count, message, pattern, *refs):
    *pieces, reply, previous, rates, loads, sums, wide, tiles = refs
    rows = PARTS * PART_ROWS
    devices = message.shape[0] // PARTS
    owners = devices // count
    groups = pieces[0].shape[1] // LANES
    halves = groups // owners
    for i in range(devices * PARTS):
        wide[i * PART_ROWS : (i + 1) * PART_ROWS, :] = message[i].astype(F32)
    step = owners * rows

    def column(row):
        return wide[pl.ds(row, count, stride=step), :]

    summary = []
    for s in range(groups):
        block = column(s)
        for b in range(1, owners):
            block = block + column(b * rows + s)
        summary.append(block.astype(BF16).astype(F32))
        sums[s] = summary[s]
    later = lax.broadcasted_iota(jnp.int32, (count, LANES), 0) > 0
    load_rows = []
    for b in range(owners):
        for h in range(halves):
            at = b * rows + groups + h
            low = jnp.where(later, column(at + halves), 0.0)
            tiles[pl.ds(b * halves + h, count, stride=groups), :] = column(at) + low
            load_rows.append(wide[at + halves : at + halves + 1, :])
    rates[...] = tiles[...].reshape(count, groups, LANES)
    loads[...] = jnp.concatenate(load_rows, axis=0)
    for piece, s in zip(pieces, piece_blocks()):
        kept = [keep(summary, [pattern[t, k] for k in range(groups)]) for t in (s, s + 1)]
        product = contract_lanes(jnp.concatenate(kept, axis=0), piece[...])
        tiles[pl.ds(s, count, stride=groups), :] = product[:count, :LANES] + sums[s]
        tiles[pl.ds(s + 1, count, stride=groups), :] = product[count:, LANES:] + sums[s + 1]
    carried = jnp.zeros((groups, LANES), F32)
    scale = loads[...]
    for r in range(count):
        previous[r] = carried
        carried = rates[r] * carried + tiles[r * groups : (r + 1) * groups, :]
        value = (scale * carried).astype(BF16)
        for b in range(owners):
            reply[r * owners + b] = value


def residual_kernel(
    sizes, phi, y, arrived, message, residuals, phi_here, weights, total, spread, sems
):
    chunks = start_chunks(sizes, ((phi, phi_here),), sems)
    traits = arrived.shape[0]
    load_by_trait(arrived, spread, weights)
    weights[traits:, :] = weights[:traits, :]
    for i, (at, copies) in enumerate(chunks):
        wait_all(copies)
        fitted = contract_lanes(weights[...], phi_here[at, :])[:traits]
        residual = (fitted - y[at, :].T.astype(F32)).astype(BF16)
        residuals[:, at] = residual
        product = jnp.dot(residual, phi_here[at, :], preferred_element_type=F32)
        if i == 0:
            total[...] = product
        else:
            total[...] += product
    store_by_trait(total[...], spread, message)


def backward_kernel(count, traits, message, pattern, previous, rates, loads, *refs):
    *pieces, reply, tiles = refs
    devices = message.shape[0]
    owners = devices // count
    groups = pieces[0].shape[1] // LANES
    halves = groups // owners
    scale = loads[...]
    adjoint = jnp.zeros((groups, LANES), F32)
    for r in reversed(range(count)):
        pulled = message[r * owners].astype(F32)
        for b in range(1, owners):
            pulled = pulled + message[r * owners + b].astype(F32)
        pulled = scale * pulled
        if r + 1 < count:
            adjoint = pulled + rates[r + 1] * adjoint
        else:
            adjoint = pulled
        tiles[r * groups : (r + 1) * groups, :] = adjoint
        slope = adjoint * previous[r] * (1.0 / traits)
        high, low = split(slope)
        high, low = high.astype(F32), low.astype(F32)
        for b in range(owners):
            mine = slice(b * halves, (b + 1) * halves)
            tail = jnp.concatenate([high[mine], low[mine]], axis=0)
            reply[(r * owners + b) * PARTS + PARTS - 1] = tail.astype(BF16)
    def block(s):
        return tiles[pl.ds(s, count, stride=groups), :].astype(BF16).astype(F32)

    blocks = [block(s) for s in range(groups)]
    firsts = piece_blocks()
    parts = [(block(s), block(s + 1)) for s in firsts]
    for s in range(0, groups, 2):
        product = jnp.zeros((2 * count, 2 * LANES), F32)
        for piece, first, part in zip(pieces, firsts, parts):
            kept = [keep(part, (pattern[first, t], pattern[first + 1, t])) for t in (s, s + 1)]
            product += jnp.dot(
                jnp.concatenate(kept, axis=0),
                piece[:, s * LANES : (s + 2) * LANES],
                preferred_element_type=F32,
            )
        tiles[pl.ds(s, count, stride=groups), :] = product[:count, :LANES] + blocks[s]
        tiles[pl.ds(s + 1, count, stride=groups), :] = product[count:, LANES:] + blocks[s + 1]
    for r in range(count):
        for part in range(PARTS - 1):
            at = r * groups + part * PART_ROWS
            back = tiles[at : at + PART_ROWS, :].astype(BF16)
            for b in range(owners):
                reply[(r * owners + b) * PARTS + part] = back


def gradient_kernel(
    sizes, halves, phi, residuals, arrived, out, slope, phi_here, out_here, weights, spread, sent, sems
):
    chunks = start_chunks(sizes, ((phi, phi_here),), sems)
    traits = residuals.shape[0]
    groups = weights.shape[1] // LANES
    for k in range(traits):
        for part in range(PARTS - 1):
            at = k * groups + part * PART_ROWS
            spread[at : at + PART_ROWS, :] = arrived[k * PARTS + part].astype(F32)
    gather_traits(spread, weights, traits, groups)
    weights[traits:, :] = weights[:traits, :]
    stores = []

    def finish(i):
        at = chunks[i][0]
        back = sent[i % 2, :, 0 : sizes[i]]
        out_here[at, :] = (back - residuals[:, at].astype(F32)).astype(BF16).T
        stores.append(pltpu.make_async_copy(out_here.at[at], out.at[at], sems.at[1, i]))
        stores[-1].start()

    for i, (at, copies) in enumerate(chunks):
        wait_all(copies)
        sent[i % 2, :, 0 : sizes[i]] = contract_lanes(weights[...], phi_here[at, :])[:traits]
        if i > 0:
            finish(i - 1)
    finish(len(chunks) - 1)
    tail = jnp.sum(arrived[pl.ds(PARTS - 1, traits, stride=PARTS)].astype(F32), axis=0)
    for h in range(halves):
        slope[:, h * LANES : (h + 1) * LANES] = (
            tail[h : h + 1, :] + tail[halves + h : halves + h + 1, :]
        )
    wait_all(stores)


def permute(value, target):
    pairs = []
    for r in range(lax.axis_size("region")):
        for b in range(OWNERS):
            to_r, to_b = target(r, b)
            pairs.append((r * OWNERS + b, to_r * OWNERS + to_b % OWNERS))
    return lax.ppermute(value, ALL, pairs)


def near_shard(mixing):
    return permute(mixing, lambda r, b: (r, b + 1 + 2 * (r % 2)))


def other_shards(near):
    swapped = permute(near, lambda r, b: (r ^ 1, b))
    across = permute(near, lambda r, b: (r ^ 1, b + 1 + 2 * (r % 2)))
    return swapped, across


def shards(count, observations, basis_values, mixing, pattern, decays, loadings):
    devices = lax.axis_size("region") * lax.axis_size("basis")
    rows, width = basis_values.shape
    traits = observations.shape[1]
    groups = width // LANES
    share = decays.shape[1]
    halves = share // LANES
    tile = min(TILE_ROWS, rows)
    even = (tile,) * (rows // tile)
    tapered = (tile // 2,) * 2 + even[2:] + (tile // 2,) * 2
    near = near_shard(mixing)

    hbm = pl.BlockSpec(memory_space=pl.ANY)
    vmem = pl.BlockSpec(memory_space=pltpu.VMEM)
    smem = pl.BlockSpec(memory_space=pltpu.SMEM)
    phi_here = pltpu.VMEM((rows, width), BF16)
    y_here = pltpu.VMEM((rows, traits), BF16)
    total = pltpu.VMEM((traits, width), F32)
    spread = pltpu.VMEM((traits * groups, LANES), F32)
    tiles = pltpu.VMEM((count * groups, LANES), F32)
    short = jax.ShapeDtypeStruct((devices, groups, LANES), BF16)
    long = jax.ShapeDtypeStruct((devices * PARTS, PART_ROWS, LANES), BF16)

    def sems(*shape):
        return pltpu.SemaphoreType.DMA(shape)

    def limit(mebibytes):
        return pltpu.CompilerParams(vmem_limit_bytes=mebibytes * MIB)

    def exchange(value):
        return lax.all_to_all(value, ALL, 0, 0, tiled=True)

    sums = pl.pallas_call(
        functools.partial(summary_kernel, tapered),
        in_specs=[hbm] * 4,
        out_specs=vmem,
        out_shape=long,
        scratch_shapes=[
            phi_here,
            y_here,
            pltpu.VMEM((1, share), F32),
            pltpu.VMEM((1, share), F32),
            total,
            spread,
            sems(2, len(tapered)),
            sems(2),
        ],
        compiler_params=limit(60),
        name="summary",
    )(basis_values, observations, decays, loadings[None, :])
    sums, near = lax.optimization_barrier((sums, near))
    pieces = (mixing, near) + other_shards(near)
    sums = exchange(sums)
    loaded, previous, rates, loads = pl.pallas_call(
        functools.partial(forward_kernel, count),
        in_specs=[vmem, smem] + [vmem] * len(pieces),
        out_specs=(vmem,) * 4,
        out_shape=(
            short,
            jax.ShapeDtypeStruct((count, groups, LANES), F32),
            jax.ShapeDtypeStruct((count, groups, LANES), F32),
            jax.ShapeDtypeStruct((groups, LANES), F32),
        ),
        scratch_shapes=[
            pltpu.VMEM((groups, count, LANES), F32),
            pltpu.VMEM((devices * PARTS * PART_ROWS, LANES), F32),
            tiles,
        ],
        compiler_params=limit(16),
        name="forward",
    )(sums, pattern, *pieces)
    loaded = exchange(loaded)
    pulled, residuals = pl.pallas_call(
        functools.partial(residual_kernel, even),
        in_specs=[hbm, vmem, vmem],
        out_specs=(vmem, vmem),
        out_shape=(short, jax.ShapeDtypeStruct((traits, rows), BF16)),
        scratch_shapes=[
            phi_here,
            pltpu.VMEM((2 * traits, width), BF16),
            total,
            spread,
            sems(1, len(even)),
        ],
        compiler_params=limit(44),
        name="residual",
    )(basis_values, observations, loaded)
    pulled = exchange(pulled)
    back = pl.pallas_call(
        functools.partial(backward_kernel, count, traits),
        in_specs=[vmem, smem, vmem, vmem, vmem] + [vmem] * len(pieces),
        out_specs=vmem,
        out_shape=long,
        scratch_shapes=[tiles],
        compiler_params=limit(16),
        name="backward",
    )(pulled, pattern, previous, rates, loads, *pieces)
    back = exchange(back)
    obs_grad, slope = pl.pallas_call(
        functools.partial(gradient_kernel, tapered, halves),
        in_specs=[hbm, vmem, vmem],
        out_specs=(hbm, vmem),
        out_shape=(
            jax.ShapeDtypeStruct((rows, traits), BF16),
            jax.ShapeDtypeStruct((1, share), F32),
        ),
        scratch_shapes=[
            phi_here,
            y_here,
            pltpu.VMEM((2 * traits, width), BF16),
            spread,
            pltpu.VMEM((2, traits, tile), F32),
            sems(2, len(tapered)),
        ],
        compiler_params=limit(44),
        name="gradient",
    )(basis_values, residuals, back)
    return obs_grad, slope


def solution(mesh):
    in_specs = (
        P(ALL, None),
        P(ALL, None),
        P("basis", None),
        P(),
        P("region", "basis"),
        P("basis"),
    )
    out_specs = (P(ALL, None), P("region", "basis"))
    body = functools.partial(shards, mesh.shape["region"])
    return jax.shard_map(body, mesh=mesh, in_specs=in_specs, out_specs=out_specs, check_vma=False)
```
